32 devices in a mesh: sample: 2 (over y), wire: 4 (over z), xsec: 2 (over x), cols: 2 (over core).
Axes of the slice: x: 2, y: 2, z: 4, core: 2. Of those that a mesh axis runs over, the one named last changes fastest.
Arguments:
- blocks: bfloat16 [32, 2, 64, 1728], P(('sample', 'wire'), 'xsec'), parts along dimension 0, may hold values from -0.109375 to 0.109375
- pattern: int32 [32, 2, 27], P(('sample', 'wire'), 'xsec'), parts along dimension 0, may hold values 0 or 1
- current: bfloat16 [32, 2, 64, 2, 512], P(('sample', 'wire'), 'xsec', None, None, 'cols'), parts along dimension 0, may hold values from -6 to 6
- previous: bfloat16 [32, 2, 64, 2, 512], P(('sample', 'wire'), 'xsec', None, None, 'cols'), parts along dimension 0, may hold values from -6 to 6
- accum: float32 [32, 2, 64, 2, 512], P(('sample', 'wire'), 'xsec', None, None, 'cols'), parts along dimension 0, may hold values from -6 to 6
- coefs: float32 [4], replicated, may hold values from 0.3 to 1
- sketch: bfloat16 [32, 2, 64, 512], P(('sample', 'wire'), 'xsec'), parts along dimension 0, may hold values from -6 to 6
- signs: int32 [32, 2, 64, 512], P(('sample', 'wire'), 'xsec', None, 'cols'), parts along dimension 0, may hold values from 0 to 1
Outputs:
- newest: bfloat16 [32, 2, 64, 2, 512], P(('sample', 'wire'), 'xsec', None, None, 'cols'), parts along dimension 0
- before: bfloat16 [32, 2, 64, 2, 512], P(('sample', 'wire'), 'xsec', None, None, 'cols'), parts along dimension 0
- summed: float32 [32, 2, 64, 2, 512], P(('sample', 'wire'), 'xsec', None, None, 'cols'), parts along dimension 0
- gram: float32 [1024, 512], P(('sample', 'wire', 'xsec'), 'cols'), parts along dimension 0
- quadratic: float32 [1024], P(('sample', 'cols')), parts along dimension 0
The draws below stay inside these ranges and needn't reach their ends.
There are 2 independent parts, one for each index of `sample`. The reference program is written for one: setup_inputs(seed, part) draws one part's arguments, and reference() takes and returns one part's arrays. A program takes and returns all parts, laid end to end along the dimension named above; an argument that names none is the same for every part. Nothing has to cross between parts.
All inputs are finite; a program needn't handle non-finite values. No bound on the sum of `pattern` on one device may be relied on, other than what follows from the above.
Results may differ from the reference program's by a relative error of at most 0.0065.
Values may be sent and summed in bfloat16 or wider, within the bound.
No kernel may reach another device: no remote copies, remote signals or barrier semaphores. Data moves between devices by JAX's collectives and lax.ppermute only.
A program may use at most 64 MiB of HBM per device.

```python
import jax
import jax.numpy as jnp
from jax import lax

ORB = 64
REACH = 4
NCOL = 512
STEPS = 4
CELLS = 16
TILES = 2
NBLK = 27


def with_ends(array, stream_key, low, high):
    spot = [jax.random.randint(jax.random.fold_in(stream_key, axis), (), 0, length) for axis, length in enumerate(array.shape)]
    longest = array.shape.index(max(array.shape))
    next_to = spot[:longest] + [(spot[longest] + 1) % array.shape[longest]] + spot[longest + 1:]
    return array.at[tuple(spot)].set(low).at[tuple(next_to)].set(high)


def strengthened(values, stream_key, source, target, blocks, factor):
    def block_of(axis_at):
        return (jnp.arange(values.shape[axis_at]) // (values.shape[axis_at] // blocks)).reshape((-1,) + (1,) * (values.ndim - 1 - axis_at))

    one_side = jax.random.permutation(stream_key, blocks)[block_of(target)]
    second = (block_of(target) + blocks // 2) % blocks
    return jnp.where((block_of(source) == one_side) | (block_of(source) == second), factor * values, values)


def level_of(stream_key, shape, cuts, smallest, top_value):
    def one(axis_at, parts):
        heights = jax.random.uniform(jax.random.fold_in(jax.random.fold_in(stream_key, 6), axis_at), (parts,), jnp.float32, smallest / len(cuts), top_value / len(cuts))
        return jnp.repeat(jnp.exp(heights), shape[axis_at] // parts).reshape((-1,) + (1,) * (len(shape) - axis_at - 1))

    level = one(*cuts[0])
    for cut in cuts[1:]:
        level = level * one(*cut)
    return level


def gaussian(rng, shape, deviation, bound, cuts=(), kind=jnp.bfloat16):
    drawn = deviation * jax.random.normal(rng, shape, jnp.float32)
    if cuts:
        drawn = drawn * level_of(rng, shape, cuts, -0.22, 0.18)
    return jnp.clip(drawn, -bound, bound).astype(kind)


def noise_with(own_key, shape, deviation, reach, split, heavy, kind=jnp.bfloat16):
    values = deviation * jax.random.normal(own_key, shape, jnp.float32)
    if split:
        values = values * level_of(own_key, shape, split, -0.22, 0.18)
    return jnp.clip(strengthened(values, jax.random.fold_in(own_key, 3), *heavy), -reach, reach).astype(kind)


def setup_inputs(seed: int = 0, part: int = 0) -> dict:
    keys = jax.random.split(jax.random.key(seed), 9)
    own_keys = jax.random.split(jax.random.fold_in(keys[8], part), 9)
    blocks = gaussian(own_keys[0], (CELLS, TILES, ORB, NBLK * ORB), (2 * NBLK * ORB) ** -0.5, 0.109375, ((0, 4), (1, 2)))
    pattern = with_ends((jax.random.randint(own_keys[1], (CELLS, TILES, NBLK), 0, 4) < 3).astype(jnp.int32), jax.random.fold_in(own_keys[1], 1), 0, 1)
    current = gaussian(own_keys[2], (CELLS, TILES, ORB, 2, NCOL), 1.0, 6.0, ((0, 4), (1, 2), (4, 2)))
    previous = gaussian(own_keys[3], (CELLS, TILES, ORB, 2, NCOL), 1.0, 6.0, ((0, 4), (1, 2), (4, 2)))
    accum = gaussian(own_keys[4], (CELLS, TILES, ORB, 2, NCOL), 1.0, 6.0, ((0, 4), (1, 2), (4, 2)), jnp.float32)
    coefs = jnp.clip(jax.random.uniform(keys[5], (STEPS,), jnp.float32, 0.3, 1.0), 0.3, 1.0)
    sketch = noise_with(own_keys[6], (CELLS, TILES, ORB, NCOL), 1.0, 6.0, ((0, 4), (1, 2)), (0, 3, 4, 2.0))
    signs = with_ends(jax.random.randint(own_keys[7], (CELLS, TILES, ORB, NCOL), 0, 2), jax.random.fold_in(own_keys[7], 1), 0, 1).astype(jnp.int32)
    return dict(blocks=blocks, pattern=pattern, current=current, previous=previous, accum=accum, coefs=coefs, sketch=sketch, signs=signs)


def apply_operator(field, blocks, pattern):
    ext = jnp.concatenate([field[-REACH:], field, field[:REACH]], axis=0)
    ext = jnp.pad(ext, ((0, 0), (1, 1), (0, 0), (0, 0), (0, 0)))

    def one_cell(cell):
        window = lax.dynamic_slice_in_dim(ext, cell, 2 * REACH + 1, 0)
        pieces = [window[d, e:e + TILES] for d in range(2 * REACH + 1) for e in range(3)]
        stack = jnp.stack(pieces, axis=1).astype(jnp.float32)
        weights = lax.dynamic_index_in_dim(pattern, cell, 0, keepdims=False).astype(jnp.float32)
        stack = stack * weights[:, :, None, None, None]
        stack = stack.reshape(TILES, NBLK * ORB, 2 * NCOL)
        rows = lax.dynamic_index_in_dim(blocks, cell, 0, keepdims=False).astype(jnp.float32)
        out = jnp.einsum('tik,tkn->tin', rows, stack)
        return out.reshape(TILES, ORB, 2, NCOL)
    return lax.map(one_cell, jnp.arange(CELLS, dtype=jnp.int32))

def reference(blocks, pattern, current, previous, accum, coefs, sketch, signs):
    for step in range(STEPS):
        image = apply_operator(current, blocks, pattern)
        nxt = (2.0 * image - previous.astype(jnp.float32)).astype(jnp.bfloat16)
        accum = accum + coefs[step] * nxt.astype(jnp.float32)
        previous = current
        current = nxt
    scale = jnp.float32(1.0) / jnp.sqrt(jnp.float32(CELLS * TILES * ORB))
    sketched = accum[:, :, :, 0, :].astype(jnp.bfloat16).reshape(CELLS * TILES * ORB, NCOL)
    omega = sketch.reshape(CELLS * TILES * ORB, NCOL)
    gram = lax.dot_general(omega, sketched, (((0,), (0,)), ((), ())), preferred_element_type=jnp.float32) * scale
    plus_minus = (2 * signs - 1).astype(jnp.float32)
    quadratic = lax.optimization_barrier(jnp.sum(plus_minus * accum[:, :, :, 1, :], axis=(0, 1, 2))) * scale
    return (current, previous, accum, gram, quadratic)
```

```python
import jax
import jax.numpy as jnp
from jax import lax
from jax.sharding import PartitionSpec as P

STEPS = 4


def from_tile(x, offset):
    size = lax.axis_size("xsec")
    return lax.ppermute(x, "xsec", [((i + offset) % size, i) for i in range(size)])


def to_tile(x, offset):
    size = lax.axis_size("xsec")
    return lax.ppermute(x, "xsec", [(i, (i + offset) % size) for i in range(size)])


def around(x, reach):
    size, cells = (lax.axis_size("wire"), x.shape[1])
    up = [(i, (i + 1) % size) for i in range(size)]
    down = [(j, i) for i, j in up]
    before = lax.ppermute(x[:, cells - reach :], "wire", up)
    after = lax.ppermute(x[:, :reach], "wire", down)
    return before, after


def column_block(x, index, width):
    return lax.dynamic_slice_in_dim(x, index * width, width, axis=x.ndim - 1)


def tiles_in(x, width):
    size, me = (lax.axis_size("xsec"), lax.axis_index("xsec"))
    parts = [column_block(x, me, width)]
    for offset in range(1, size):
        parts.append(from_tile(column_block(x, (me - offset) % size, width), offset))
    return parts


def columns_out(parts):
    size, me = (lax.axis_size("xsec"), lax.axis_index("xsec"))
    got = [parts[0]] + [to_tile(parts[offset], offset) for offset in range(1, size)]
    blocks = []
    for j in range(size):
        block = got[0]
        for offset in range(1, size):
            block = jnp.where((me - offset) % size == j, got[offset], block)
        blocks.append(block)
    return jnp.concatenate(blocks, axis=-1)


def band_of(masked, pairs, reach):
    size, me = (lax.axis_size("xsec"), lax.axis_index("xsec"))
    rows = []
    for i in range(size):
        cells = masked[i].shape[0]
        columns = []
        for u in range(size):
            gap = (me + u) % size - (me + i) % size + 1
            picked = lax.dynamic_index_in_dim(masked[i], jnp.clip(gap, 0, 2), 3, keepdims=False)
            if size > 2 and i != u:
                picked = jnp.where((gap >= 0) & (gap <= 2), picked, jnp.zeros_like(picked))
            band = jnp.stack(
                [jnp.pad(picked[c], ((0, 0), (c, cells - 1 - c), (0, 0))) for c in range(cells)]
            )
            columns.append(band)
        rows.append(columns)
    ext = cells + 2 * reach
    orbs = masked[0].shape[1]

    def part(low, high):
        return jnp.concatenate(
            [
                jnp.concatenate(
                    [b[:, :, low:high].reshape(cells * orbs, (high - low) * orbs) for b in columns],
                    axis=1,
                )
                for columns in rows
            ],
            axis=0,
        )

    return part(0, reach), part(reach, reach + cells), part(reach + cells, ext)


def body(blocks, pattern, current, previous, accum, coefs, sketch, signs):
    cells, tiles, orbs, wide = blocks.shape
    halves, local_cols = current.shape[3:]
    count = wide // orbs
    span = count // 3
    reach = span // 2
    xs, me = (lax.axis_size("xsec"), lax.axis_index("xsec"))
    wires = lax.axis_size("wire")
    width = local_cols // xs
    rows = cells * orbs

    field_parts = tiles_in(current[:, 0], width)
    halo_parts = [around(f[None].reshape(1, cells, orbs, halves * width), reach) for f in field_parts]

    masked = (
        blocks[:, 0].reshape(cells, orbs, count, orbs)
        * pattern[:, 0].astype(jnp.bfloat16)[:, None, :, None]
    ).reshape(cells, orbs, span, 3, orbs)
    everyone = [masked] + [from_tile(masked, offset) for offset in range(1, xs)]
    left, own, right = band_of(everyone, None, reach)

    field = [jnp.stack([f[:, :, h] for f in field_parts]) for h in range(halves)]
    before_parts = tiles_in(previous[:, 0], width)
    older = [jnp.stack([f[:, :, h] for f in before_parts]) for h in range(halves)]
    accum_parts = tiles_in(accum[:, 0], width)
    total = [jnp.stack([f[:, :, h] for f in accum_parts]) for h in range(halves)]
    omega_parts = [sketch[:, 0]] + [from_tile(sketch[:, 0], offset) for offset in range(1, xs)]
    omega = jnp.stack(omega_parts).reshape(xs * rows, sketch.shape[3])
    sign_parts = tiles_in((2 * signs[:, 0] - 1).astype(jnp.bfloat16), width)
    plus_minus = jnp.stack(sign_parts)

    halo = [
        [
            jnp.concatenate(
                [p[side].reshape(1, reach, orbs, halves, width)[:, :, :, h] for p in halo_parts]
            )
            for side in range(2)
        ]
        for h in range(halves)
    ]

    def dot(matrix, value):
        return lax.dot(
            matrix, value.reshape(matrix.shape[1], width), preferred_element_type=jnp.float32
        )

    partial_sum = [None] * halves
    for step in range(STEPS):
        for h in range(halves):
            if step > 0:
                halo[h] = around(field[h], reach)
            image = dot(own, field[h]) + dot(left, halo[h][0]) + dot(right, halo[h][1])
            image = image.reshape(xs, cells, orbs, width)
            nxt = (2.0 * image - older[h].astype(jnp.float32)).astype(jnp.bfloat16)
            partial_sum[h] = total[h]
            total[h] = total[h] + coefs[step] * nxt.astype(jnp.float32)
            older[h] = field[h]
            field[h] = nxt

    newest = jnp.stack(
        [columns_out([field[h][i] for i in range(xs)]) for h in range(halves)], axis=2
    )
    before = jnp.stack(
        [columns_out([older[h][i] for i in range(xs)]) for h in range(halves)], axis=2
    )
    summed = jnp.stack(
        [columns_out([partial_sum[h][i] for i in range(xs)]) for h in range(halves)], axis=2
    )
    summed = summed + coefs[STEPS - 1] * newest.astype(jnp.float32)

    all_rows = cells * wires * tiles * xs * orbs
    scale = jnp.float32(1.0) / jnp.sqrt(jnp.float32(all_rows))

    sketched = total[0].astype(jnp.bfloat16).reshape(xs * rows, width)
    piece = lax.dot_general(
        omega, sketched, (((0,), (0,)), ((), ())), preferred_element_type=jnp.float32
    )
    place = lax.axis_index("wire")
    piece = piece.reshape((wires, piece.shape[0] // wires, width))
    hop = 1
    while hop < wires:
        split = piece.reshape((-1, 2) + piece.shape[1:])
        bit = (place // hop) % 2
        keep = lax.dynamic_index_in_dim(split, bit, 1, keepdims=False)
        send = lax.dynamic_index_in_dim(split, 1 - bit, 1, keepdims=False)
        got = lax.ppermute(
            send.astype(jnp.bfloat16), "wire", [(i, i ^ hop) for i in range(wires)]
        )
        piece = keep + got.astype(jnp.float32)
        hop *= 2
    piece = piece[0] * scale
    piece = piece.reshape((xs, piece.shape[0] // xs, width))
    gram = columns_out(
        [lax.dynamic_index_in_dim(piece, (me + i) % xs, 0, keepdims=False) for i in range(xs)]
    )

    quad = jnp.sum(plus_minus.astype(jnp.float32) * total[1], axis=(0, 1, 2))[None]
    hop = 1
    while hop < wires:
        quad = quad + lax.ppermute(quad, "wire", [(i, i ^ hop) for i in range(wires)])
        hop *= 2
    quad = quad * scale
    quadratic = columns_out([quad] * xs)[0]

    return (newest[:, None], before[:, None], summed[:, None], gram, quadratic)


def solution(mesh):
    return jax.shard_map(
        body,
        mesh=mesh,
        in_specs=(
            P(("sample", "wire"), "xsec", None, None),
            P(("sample", "wire"), "xsec", None),
            P(("sample", "wire"), "xsec", None, None, "cols"),
            P(("sample", "wire"), "xsec", None, None, "cols"),
            P(("sample", "wire"), "xsec", None, None, "cols"),
            P(),
            P(("sample", "wire"), "xsec", None, None),
            P(("sample", "wire"), "xsec", None, "cols"),
        ),
        out_specs=(
            P(("sample", "wire"), "xsec", None, None, "cols"),
            P(("sample", "wire"), "xsec", None, None, "cols"),
            P(("sample", "wire"), "xsec", None, None, "cols"),
            P(("sample", "wire", "xsec"), "cols"),
            P(("sample", "cols")),
        ),
        check_vma=False,
    )
```

```python
import functools

import jax
import jax.numpy as jnp
from jax import lax
from jax.experimental import pallas as pl
from jax.experimental.pallas import tpu as pltpu
from jax.sharding import PartitionSpec as P

STEPS = 4
VMEM = 12 << 20
SCALAR = pl.BlockSpec(memory_space=pltpu.SMEM)
WHOLE = pl.BlockSpec(memory_space=pltpu.VMEM)
PARAMS = pltpu.CompilerParams(vmem_limit_bytes=VMEM)


def bf16(*shape):
    return jax.ShapeDtypeStruct(shape, jnp.bfloat16)


def f32(*shape):
    return jax.ShapeDtypeStruct(shape, jnp.float32)


def cost(moved, flops=0):
    return pl.CostEstimate(flops=flops, transcendentals=0, bytes_accessed=moved)


def from_tile(x, offset, axis="xsec"):
    size = lax.axis_size(axis)
    return lax.ppermute(x, axis, [((i + offset) % size, i) for i in range(size)])


def to_tile(x, offset):
    return from_tile(x, lax.axis_size("xsec") - offset)


def around(x):
    size = lax.axis_size("wire")
    first, second = ([], [])
    for i in range(0, size, 2):
        j, k = (i + 1, (i + 2) % size)
        first += [(i, j), (j, i)]
        second += [(j, k), (k, j)]
    one = lax.ppermute(x, "wire", first)
    two = lax.ppermute(x, "wire", second)
    return one, two


def swap_bits(x, hop):
    return lax.ppermute(x, "wire", [(i, i ^ hop) for i in range(lax.axis_size("wire"))])


def deal_kernel(me, x, *outs):
    cells, _, orbs, halves, columns = x.shape
    count = len(outs)
    width = columns // count
    wide = x[...].astype(jnp.float32)
    for h in range(halves):
        value = wide[:, 0, :, h, :].reshape(cells * orbs, columns)
        for i in range(count):
            picked = value[:, :width]
            for b in range(1, count):
                block = value[:, b * width : (b + 1) * width]
                picked = jnp.where((me[0] - i + count) % count == b, block, picked)
            outs[i][:, h * width : (h + 1) * width] = picked.astype(x.dtype)


def deal(x, me):
    count = lax.axis_size("xsec")
    cells, _, orbs, halves, columns = x.shape
    shape = (cells * orbs, halves * columns // count)
    return pl.pallas_call(
        deal_kernel,
        out_shape=[jax.ShapeDtypeStruct(shape, x.dtype)] * count,
        in_specs=[SCALAR, WHOLE],
        out_specs=[WHOLE] * count,
        compiler_params=PARAMS,
        cost_estimate=cost(2 * x.size * x.dtype.itemsize),
    )(me, x)


def before_kernel(count, me, *refs):
    out = refs[-1]
    cells, _, orbs, halves, columns = out.shape
    width = columns // count
    rows = cells * orbs
    for h in range(halves):
        own, got = (refs[h * count], refs[h * count + 1 : (h + 1) * count])
        for b in range(count):
            value = own[:rows].astype(jnp.float32)
            for i in range(1, count):
                other = got[i - 1][...].astype(jnp.float32)
                value = jnp.where((me[0] - i + count) % count == b, other, value)
            value = value.astype(out.dtype).reshape(cells, orbs, width)
            out[:, 0, :, h, b * width : (b + 1) * width] = value


def last_kernel(count, me, coef, *refs):
    newest, summed = refs[-2:]
    cells, _, orbs, halves, columns = newest.shape
    width = columns // count
    rows = cells * orbs
    for h in range(halves):
        at = h * 3 * count

        def value(kind, i):
            return refs[at + kind * count + i][:rows].astype(jnp.float32)

        for b in range(count):
            late, mid, sums = [value(kind, 0) for kind in range(3)]
            for i in range(1, count):
                here = (me[0] - i + count) % count == b
                late = jnp.where(here, value(0, i), late)
                mid = jnp.where(here, value(1, i), mid)
                sums = jnp.where(here, value(2, i), sums)
            columns_at = slice(b * width, (b + 1) * width)
            shape = (cells, orbs, width)
            newest[:, 0, :, h, columns_at] = late.astype(newest.dtype).reshape(shape)
            sums = sums + coef[STEPS - 2] * mid
            sums = sums + coef[STEPS - 1] * late
            summed[:, 0, :, h, columns_at] = sums.reshape(shape)


def band_kernel(tile, sizes, gap, even, slot, pattern, *refs):
    cells, orbs, reach, tiles, pieces = sizes
    first, own, second = refs[-3:]
    share = cells // pieces
    span = 2 * reach + 1
    zero = jnp.zeros((orbs, orbs), jnp.bfloat16)

    def write(parts):
        def block(c, u, x):
            d = x - c
            if d < 0 or d >= span:
                return zero
            ref = parts[c // share]

            def at(e):
                column = 3 * d + e
                value = ref[c % share, :, column * orbs : (column + 1) * orbs]
                wanted = pattern[c, column] != 0
                if u != tile:
                    wanted = wanted & (gap[u] == e)
                return value, wanted

            if u == tile:
                value, wanted = at(1)
                return jnp.where(wanted, value, zero)
            low, want_low = at(0)
            high, want_high = at(2)
            return jnp.where(want_low, low, jnp.where(want_high, high, zero))

        turn = even[0] != 0
        for c in range(cells):
            rows = slice(c * orbs, (c + 1) * orbs)
            for u in range(tiles):
                for j in range(cells):
                    at = (u * cells + j) * orbs
                    own[rows, at : at + orbs] = block(c, u, reach + j)
                for j in range(reach):
                    at = (u * reach + j) * orbs
                    left, right = (block(c, u, j), block(c, u, reach + cells + j))
                    first[rows, at : at + orbs] = jnp.where(turn, right, left)
                    second[rows, at : at + orbs] = jnp.where(turn, left, right)

    for k in range(pieces):

        @pl.when(slot[0] == k)
        def _():
            write([refs[(piece - k) % pieces] for piece in range(pieces)])


def band_rows(tile, parts, pattern, gap, even, slot, sizes, held):
    cells, orbs, reach, tiles, _ = sizes
    rows = cells * orbs
    shapes = [(tiles * rows, tiles * n * orbs) for n in (reach, cells, reach)]
    n_in = 4 + len(parts)
    return pl.pallas_call(
        functools.partial(band_kernel, tile, sizes),
        out_shape=[bf16(*s) for s in shapes],
        grid=(1,),
        in_specs=[SCALAR] * 4
        + [pl.BlockSpec(p.shape, lambda i: (0, 0, 0)) for p in parts]
        + [pl.BlockSpec(memory_space=pl.ANY)] * len(held),
        out_specs=[pl.BlockSpec((rows, s[1]), lambda i: (tile, 0)) for s in shapes],
        input_output_aliases={n_in + i: i for i in range(len(held))},
        compiler_params=PARAMS,
        cost_estimate=cost(4 * rows * tiles * 3 * cells * orbs),
    )(gap, even, slot, pattern, *parts, *held)


def step_kernel(step, width, counts, lanes, kind, info, coef, *refs):
    refs = list(refs)

    def take(n):
        taken = refs[:n]
        del refs[:n]
        return taken

    own, first, second = take(3)
    field, near, far, older, sums, extra = [take(n) for n in counts]

    def parts(group, lane):
        return [ref[:, lane : lane + width] for ref in group]

    image = None
    for band, group, lane in zip((own, first, second), (field, near, far), lanes):
        at = 0
        for value in parts(group, lane[0]):
            depth = value.shape[0]
            term = jnp.dot(
                band[:, at : at + depth], value, preferred_element_type=jnp.float32
            )
            image = term if image is None else image + term
            at += depth

    old = jnp.concatenate(parts(older, lanes[3][0]))
    value = (2.0 * image - old.astype(jnp.float32)).astype(jnp.bfloat16)
    outs = refs
    size = value.shape[0]

    if kind in ("plain", "sum", "before"):
        outs.pop(0)[...] = value
    if kind in ("sum", "sketch", "probe"):
        now = jnp.concatenate(parts(field, lanes[0][0])).astype(jnp.float32)
        total = jnp.concatenate(parts(sums, lanes[4][0]))
        total = total + coef[step - 1] * now
        total = total + coef[step] * value.astype(jnp.float32)
    if kind == "sum":
        tiles = len(outs)
        for i in range(tiles):
            outs[i][...] = total[i * (size // tiles) : (i + 1) * (size // tiles)]
    if kind == "before":
        tiles = len(outs) + 1
        for i in range(1, tiles):
            outs[i - 1][...] = value[i * (size // tiles) : (i + 1) * (size // tiles)]
    if kind in ("sketch", "probe"):
        tiles = len(extra)
        for i in range(tiles):
            outs.pop(0)[...] = value[i * (size // tiles) : (i + 1) * (size // tiles)]
    if kind == "sketch":
        sketched = total.astype(jnp.bfloat16)
        piece = None
        for i, omega in enumerate(extra):
            term = jnp.dot(
                omega[...],
                sketched[i * (size // tiles) : (i + 1) * (size // tiles)],
                preferred_element_type=jnp.float32,
            )
            piece = term if piece is None else piece + term
        keep, send = outs
        high = keep.shape[1]
        for q in range(keep.shape[0]):
            low = piece[2 * q * high : (2 * q + 1) * high]
            top = piece[(2 * q + 1) * high : (2 * q + 2) * high]
            odd = info[0] % 2 == 1
            keep[q] = jnp.where(odd, top, low)
            send[q] = jnp.where(odd, low, top).astype(jnp.bfloat16)
    if kind == "probe":
        signs = jnp.concatenate([ref[...] for ref in extra]).astype(jnp.float32)
        outs[0][...] = jnp.sum(signs * total, axis=0, keepdims=True)


def advance(step, width, kind, info, coef, band, groups, lanes, outs):
    flat = [x for group in groups for x in group]
    rows, depth = band[1].shape
    return pl.pallas_call(
        functools.partial(step_kernel, step, width, [len(group) for group in groups], lanes, kind),
        out_shape=outs,
        in_specs=[SCALAR] * 2 + [WHOLE] * (3 + len(flat)),
        out_specs=[WHOLE] * len(outs),
        compiler_params=PARAMS,
        cost_estimate=cost(6 * rows * depth, 6 * rows * depth * width),
    )(info, coef, band[1], band[0], band[2], *flat)


def program(blocks, pattern, current, previous, accum, coefs, sketch, signs):
    cells, tiles, orbs, wide = blocks.shape
    halves, local_cols = current.shape[3:]
    reach = wide // orbs // 6
    xs, me = (lax.axis_size("xsec"), lax.axis_index("xsec").astype(jnp.int32))
    wires, place = (lax.axis_size("wire"), lax.axis_index("wire").astype(jnp.int32))
    cores, core = (lax.axis_size("cols"), lax.axis_index("cols").astype(jnp.int32))
    width = local_cols // xs
    rows = cells * orbs
    others = range(1, xs)
    assert tiles == 1 and cells == reach and wires % 2 == 0 and cells % cores == 0
    assert halves == 2 and STEPS == 4

    def column_block(x, i):
        return lax.dynamic_slice_in_dim(x, (me - i) % xs * width, width, axis=x.ndim - 1)

    blocks = blocks[:, 0]
    pattern = pattern[:, 0]
    share = cells // cores
    mine = lax.dynamic_slice_in_dim(blocks, core * share, share, axis=0)
    shares = [from_tile(mine, i) for i in others]
    patterns = [pattern] + [from_tile(pattern, i) for i in others]

    by_half = [current[:, 0, :, h].reshape(rows, local_cols) for h in range(halves)]
    dealt = [
        jnp.concatenate([column_block(v, i) for v in by_half], axis=1) for i in range(xs)
    ]
    field = [dealt[0]] + [from_tile(dealt[i], i) for i in others]
    halo = [around(field[0])]
    halo += [around(field[i]) for i in others]

    even = (1 - place % 2)[None]
    band = ()
    for i in range(xs):
        parts, slot, pieces = ([blocks], jnp.zeros((1,), jnp.int32), 1)
        if i > 0:
            parts = [shares[i - 1]]
            parts += [from_tile(shares[i - 1], k, "cols") for k in range(1, cores)]
            slot, pieces = (core[None], cores)
        gap = (me + lax.iota(jnp.int32, xs)) % xs - (me + i) % xs + 1
        sizes = (cells, orbs, reach, xs, pieces)
        band = band_rows(i, parts, patterns[i], gap, even, slot, sizes, band)

    dealt = deal(previous, me[None])
    older = [dealt[0]] + [from_tile(dealt[i], i) for i in others]
    dealt = deal(accum, me[None])
    sums = [dealt[0]] + [from_tile(dealt[i], i) for i in others]
    omega = sketch[:, 0].reshape(rows, sketch.shape[3]).T
    omega = [omega] + [from_tile(omega, i) for i in others]
    signed = (2 * signs[:, 0] - 1).astype(jnp.bfloat16).reshape(rows, local_cols)
    signed = [column_block(signed, 0)] + [from_tile(column_block(signed, i), i) for i in others]

    ranks = sketch.shape[3]
    full = bf16(xs * rows, width)
    piece = bf16(rows, width)
    info = place[None]

    def run(step, kind, field, near, far, older, sums, extra, lanes, outs):
        return advance(
            step, width, kind, info, coefs, band,
            (field, near, far, older, sums, extra), lanes, outs,
        )

    fields, olders, totals = ([None] * halves, [None] * halves, [None] * halves)
    for h in range(halves):
        lane = h * width
        (fields[h],) = run(
            0, "plain", field, [p[0] for p in halo], [p[1] for p in halo], older, [], [],
            ((lane,), (lane,), (lane,), (lane,), ()), [full],
        )
    zero = (0,)
    for h in range(halves):
        lane = (h * width,)
        near, far = around(fields[h])
        nxt, *totals[h] = run(
            1, "sum", [fields[h]], [near], [far], field, sums, [],
            (zero, zero, zero, lane, lane), [full] + [f32(rows, width)] * xs,
        )
        olders[h], fields[h] = (fields[h], nxt)
    befores = [None] * halves
    for h in range(halves):
        near, far = around(fields[h])
        nxt, *befores[h] = run(
            2, "before", [fields[h]], [near], [far], [olders[h]], [], [],
            (zero, zero, zero, zero, ()), [full] + [piece] * (xs - 1),
        )
        olders[h], fields[h] = (fields[h], nxt)
    newest, extras = ([None] * halves, [None] * halves)
    part = (wires // 2, ranks // wires, width)
    ends = [("sketch", omega, [f32(*part), bf16(*part)]), ("probe", signed, [f32(1, width)])]
    for h in range(halves):
        near, far = around(fields[h])
        kind, extra, outs = ends[h]
        results = run(
            3, kind, [fields[h]], [near], [far], [olders[h]], totals[h], extra,
            (zero, zero, zero, zero, zero), [piece] * xs + outs,
        )
        newest[h], extras[h] = (results[:xs], results[xs:])
    (keep, send), (quad,) = extras

    scale = jnp.float32(1.0) / jnp.sqrt(jnp.float32(rows * wires * tiles * xs))
    hop = 1
    while True:
        summed = keep + swap_bits(send, hop).astype(jnp.float32)
        hop *= 2
        if hop == wires:
            break
        split = summed.reshape((-1, 2) + summed.shape[1:])
        bit = (place // hop) % 2
        keep = lax.dynamic_index_in_dim(split, bit, 1, keepdims=False)
        send = lax.dynamic_index_in_dim(split, 1 - bit, 1, keepdims=False).astype(jnp.bfloat16)
    summed = summed[0] * scale
    summed = summed.reshape((xs, summed.shape[0] // xs, width))

    def placed(parts):
        got = [parts[0]] + [to_tile(parts[i], i) for i in others]
        blocks = []
        for b in range(xs):
            block = got[0]
            for i in others:
                block = jnp.where((me - i) % xs == b, got[i], block)
            blocks.append(block)
        return jnp.concatenate(blocks, axis=-1)

    gram = placed(
        [lax.dynamic_index_in_dim(summed, (me + i) % xs, 0, keepdims=False) for i in range(xs)],
    )

    hop = 1
    while hop < wires:
        quad = quad + sum(swap_bits(quad, hop * k) for k in range(1, min(4, wires // hop)))
        hop *= 4
    quadratic = placed([quad * scale] * xs)[0]

    sums_back = [[totals[h][0]] + [to_tile(totals[h][i], i) for i in others] for h in range(halves)]
    before_back = [
        [fields[h]] + [to_tile(befores[h][i - 1], i) for i in others]
        for h in range(halves)
    ]
    newest_back = [
        [newest[h][0]] + [to_tile(newest[h][i], i) for i in others]
        for h in range(halves)
    ]
    shape = current.shape
    before = pl.pallas_call(
        functools.partial(before_kernel, xs),
        out_shape=bf16(*shape),
        in_specs=[SCALAR] + [WHOLE] * (halves * xs),
        out_specs=WHOLE,
        compiler_params=PARAMS,
        cost_estimate=cost(4 * current.size),
    )(me[None], *before_back[0], *before_back[1])
    flat = [x for h in range(halves) for x in newest_back[h] + before_back[h] + sums_back[h]]
    last, total = pl.pallas_call(
        functools.partial(last_kernel, xs),
        out_shape=[bf16(*shape), f32(*shape)],
        in_specs=[SCALAR, SCALAR] + [WHOLE] * len(flat),
        out_specs=[WHOLE, WHOLE],
        compiler_params=PARAMS,
        cost_estimate=cost(16 * current.size),
    )(me[None], coefs, *flat)
    return (last, before, total, gram, quadratic)


def solution(mesh):
    return jax.shard_map(
        program,
        mesh=mesh,
        in_specs=(
            P(("sample", "wire"), "xsec", None, None),
            P(("sample", "wire"), "xsec", None),
            P(("sample", "wire"), "xsec", None, None, "cols"),
            P(("sample", "wire"), "xsec", None, None, "cols"),
            P(("sample", "wire"), "xsec", None, None, "cols"),
            P(),
            P(("sample", "wire"), "xsec", None, None),
            P(("sample", "wire"), "xsec", None, "cols"),
        ),
        out_specs=(
            P(("sample", "wire"), "xsec", None, None, "cols"),
            P(("sample", "wire"), "xsec", None, None, "cols"),
            P(("sample", "wire"), "xsec", None, None, "cols"),
            P(("sample", "wire", "xsec"), "cols"),
            P(("sample", "cols")),
        ),
        check_vma=False,
    )
```

```python
import functools

import jax
import jax.numpy as jnp
from jax import lax
from jax.experimental import pallas as pl
from jax.experimental.pallas import tpu as pltpu
from jax.sharding import PartitionSpec as P

STEPS = 4
VMEM = 12 << 20
SCALAR = pl.BlockSpec(memory_space=pltpu.SMEM)
WHOLE = pl.BlockSpec(memory_space=pltpu.VMEM)
PARAMS = pltpu.CompilerParams(vmem_limit_bytes=VMEM)


def bf16(*shape):
    return jax.ShapeDtypeStruct(shape, jnp.bfloat16)


def f32(*shape):
    return jax.ShapeDtypeStruct(shape, jnp.float32)


def cost(moved, flops=0):
    return pl.CostEstimate(flops=flops, transcendentals=0, bytes_accessed=moved)


def from_tile(x, offset, axis="xsec"):
    size = lax.axis_size(axis)
    return lax.ppermute(x, axis, [((i + offset) % size, i) for i in range(size)])


def to_tile(x, offset):
    return from_tile(x, lax.axis_size("xsec") - offset)


def around(x):
    size = lax.axis_size("wire")
    first, second = ([], [])
    for i in range(0, size, 2):
        j, k = (i + 1, (i + 2) % size)
        first += [(i, j), (j, i)]
        second += [(j, k), (k, j)]
    one = lax.ppermute(x, "wire", first)
    two = lax.ppermute(x, "wire", second)
    return one, two


def swap_bits(x, hop):
    return lax.ppermute(x, "wire", [(i, i ^ hop) for i in range(lax.axis_size("wire"))])


def deal_kernel(me, x, *outs):
    cells, _, orbs, halves, columns = x.shape
    count = len(outs)
    width = columns // count
    wide = x[...].astype(jnp.float32)
    for h in range(halves):
        value = wide[:, 0, :, h, :].reshape(cells * orbs, columns)
        for i in range(count):
            picked = value[:, :width]
            for b in range(1, count):
                block = value[:, b * width : (b + 1) * width]
                picked = jnp.where((me[0] - i + count) % count == b, block, picked)
            outs[i][:, h * width : (h + 1) * width] = picked.astype(x.dtype)


def deal(x, me):
    count = lax.axis_size("xsec")
    cells, _, orbs, halves, columns = x.shape
    shape = (cells * orbs, halves * columns // count)
    return pl.pallas_call(
        deal_kernel,
        out_shape=[jax.ShapeDtypeStruct(shape, x.dtype)] * count,
        in_specs=[SCALAR, WHOLE],
        out_specs=[WHOLE] * count,
        compiler_params=PARAMS,
        cost_estimate=cost(2 * x.size * x.dtype.itemsize),
    )(me, x)


def stack_kernel(*refs):
    count = refs[-1].shape[0] // refs[0].shape[0]
    ins, outs = (refs[:count], refs[count:])
    rows, width = (ins[0].shape[0], outs[0].shape[1])
    for h, out in enumerate(outs):
        for i, ref in enumerate(ins):
            out[i * rows : (i + 1) * rows] = ref[:, h * width : (h + 1) * width]


def stacked(parts, width):
    rows, columns = parts[0].shape
    shape = bf16(len(parts) * rows, width)
    return pl.pallas_call(
        stack_kernel,
        out_shape=[shape] * (columns // width),
        in_specs=[WHOLE] * len(parts),
        out_specs=[WHOLE] * (columns // width),
        compiler_params=PARAMS,
        cost_estimate=cost(4 * len(parts) * rows * columns),
    )(*parts)


def rest_kernel(me, sketch, signs, turned, *outs):
    cells, _, orbs, ranks = sketch.shape
    count = len(outs)
    columns = signs.shape[3]
    width = columns // count
    value = sketch[...].reshape(cells * orbs, ranks)
    turned[...] = value.astype(jnp.float32).T.astype(jnp.bfloat16)
    value = (2 * signs[...] - 1).astype(jnp.float32).reshape(cells * orbs, columns)
    for i in range(count):
        picked = value[:, :width]
        for b in range(1, count):
            block = value[:, b * width : (b + 1) * width]
            picked = jnp.where((me[0] - i + count) % count == b, block, picked)
        outs[i][...] = picked.astype(jnp.bfloat16)


def before_kernel(count, me, *refs):
    out = refs[-1]
    cells, _, orbs, halves, columns = out.shape
    width = columns // count
    rows = cells * orbs
    for h in range(halves):
        own, got = (refs[h * count], refs[h * count + 1 : (h + 1) * count])
        for b in range(count):
            value = own[:rows].astype(jnp.float32)
            for i in range(1, count):
                other = got[i - 1][...].astype(jnp.float32)
                value = jnp.where((me[0] - i + count) % count == b, other, value)
            value = value.astype(out.dtype).reshape(cells, orbs, width)
            out[:, 0, :, h, b * width : (b + 1) * width] = value


def last_kernel(count, me, coef, *refs):
    newest, summed = refs[-2:]
    cells, _, orbs, halves, columns = newest.shape
    width = columns // count
    rows = cells * orbs
    for h in range(halves):
        at = h * 3 * count

        def value(kind, i):
            return refs[at + kind * count + i][:rows].astype(jnp.float32)

        for b in range(count):
            late, mid, sums = [value(kind, 0) for kind in range(3)]
            for i in range(1, count):
                here = (me[0] - i + count) % count == b
                late = jnp.where(here, value(0, i), late)
                mid = jnp.where(here, value(1, i), mid)
                sums = jnp.where(here, value(2, i), sums)
            columns_at = slice(b * width, (b + 1) * width)
            shape = (cells, orbs, width)
            newest[:, 0, :, h, columns_at] = late.astype(newest.dtype).reshape(shape)
            sums = sums + coef[STEPS - 2] * mid
            sums = sums + coef[STEPS - 1] * late
            summed[:, 0, :, h, columns_at] = sums.reshape(shape)


def pack_kernel(core, me, pattern, blocks, out):
    share, orbs, wide = blocks.shape
    span = wide // orbs // 3
    slots = out.shape[2] // orbs // span
    zero = jnp.zeros((orbs, orbs), jnp.bfloat16)
    for c in range(share):
        cell = core[0] * share + c

        def block(d, e):
            column = 3 * d + e
            value = blocks[c, :, column * orbs : (column + 1) * orbs]
            return jnp.where(pattern[cell, column] != 0, value, zero)

        for d in range(span):
            values = [block(d, e) for e in range(3)]
            if slots == 2:
                values = [values[1], jnp.where(me[0] == 0, values[2], values[0])]
            for n, value in enumerate(values):
                at = (slots * d + n) * orbs
                out[c, :, at : at + orbs] = value


def packed(blocks, pattern, core, me, cores, slots):
    cells, orbs, wide = blocks.shape
    share = cells // cores
    shape = (share, orbs, wide // 3 * slots)
    return pl.pallas_call(
        pack_kernel,
        out_shape=bf16(*shape),
        grid_spec=pltpu.PrefetchScalarGridSpec(
            num_scalar_prefetch=3,
            grid=(1,),
            in_specs=[pl.BlockSpec((share, orbs, wide), lambda i, core, me, p: (core[0], 0, 0))],
            out_specs=pl.BlockSpec(shape, lambda i, core, me, p: (0, 0, 0)),
        ),
        compiler_params=PARAMS,
        cost_estimate=cost(4 * share * orbs * wide),
    )(core, me, pattern, blocks)


def band_kernel(tile, sizes, gap, even, slot, pattern, *refs):
    cells, orbs, reach, tiles, pieces = sizes
    first, own, second = refs[-3:]
    share = cells // pieces
    span = 2 * reach + 1
    zero = jnp.zeros((orbs, orbs), jnp.bfloat16)
    slots = refs[0].shape[2] // orbs // span
    masked = tile == 0

    def write(parts):
        def block(c, u, x):
            d = x - c
            if d < 0 or d >= span:
                return zero
            ref = parts[c // share]

            def at(e):
                column = slots * d + e
                value = ref[c % share, :, column * orbs : (column + 1) * orbs]
                if masked:
                    value = jnp.where(pattern[c, column] != 0, value, zero)
                return value

            if slots == 2:
                return at(0 if u == tile else 1)
            if u == tile:
                return at(1)
            return jnp.where(gap[u] == 0, at(0), jnp.where(gap[u] == 2, at(2), zero))

        turn = even[0] != 0
        for c in range(cells):
            rows = slice(c * orbs, (c + 1) * orbs)
            for u in range(tiles):
                for j in range(cells):
                    at = (u * cells + j) * orbs
                    own[rows, at : at + orbs] = block(c, u, reach + j)
                for j in range(reach):
                    at = (u * reach + j) * orbs
                    left, right = (block(c, u, j), block(c, u, reach + cells + j))
                    first[rows, at : at + orbs] = jnp.where(turn, right, left)
                    second[rows, at : at + orbs] = jnp.where(turn, left, right)

    for k in range(pieces):

        @pl.when(slot[0] == k)
        def _():
            write([refs[(piece - k) % pieces] for piece in range(pieces)])


def band_rows(tile, parts, pattern, gap, even, slot, sizes, held):
    cells, orbs, reach, tiles, _ = sizes
    rows = cells * orbs
    shapes = [(tiles * rows, tiles * n * orbs) for n in (reach, cells, reach)]
    n_in = 4 + len(parts)
    return pl.pallas_call(
        functools.partial(band_kernel, tile, sizes),
        out_shape=[bf16(*s) for s in shapes],
        grid=(1,),
        in_specs=[SCALAR] * 4
        + [pl.BlockSpec(p.shape, lambda i: (0, 0, 0)) for p in parts]
        + [pl.BlockSpec(memory_space=pl.ANY)] * len(held),
        out_specs=[pl.BlockSpec((rows, s[1]), lambda i: (tile, 0)) for s in shapes],
        input_output_aliases={n_in + i: i for i in range(len(held))},
        compiler_params=PARAMS,
        cost_estimate=cost(4 * rows * tiles * 3 * cells * orbs),
    )(gap, even, slot, pattern, *parts, *held)


def step_kernel(step, width, counts, lanes, kind, info, coef, *refs):
    refs = list(refs)

    def take(n):
        taken = refs[:n]
        del refs[:n]
        return taken

    own, first, second = take(3)
    field, near, far, older, sums, extra = [take(n) for n in counts]

    def parts(group, lane):
        return [ref[:, lane : lane + width] for ref in group]

    image = None
    for band, group, lane in zip((own, first, second), (field, near, far), lanes):
        at = 0
        for value in parts(group, lane[0]):
            depth = value.shape[0]
            term = jnp.dot(
                band[:, at : at + depth], value, preferred_element_type=jnp.float32
            )
            image = term if image is None else image + term
            at += depth

    old = jnp.concatenate(parts(older, lanes[3][0]))
    value = (2.0 * image - old.astype(jnp.float32)).astype(jnp.bfloat16)
    outs = refs
    size = value.shape[0]

    if kind in ("plain", "sum", "before"):
        outs.pop(0)[...] = value
    if kind in ("sum", "sketch", "probe"):
        now = jnp.concatenate(parts(field, lanes[0][0])).astype(jnp.float32)
        total = jnp.concatenate(parts(sums, lanes[4][0]))
        total = total + coef[step - 1] * now
        total = total + coef[step] * value.astype(jnp.float32)
    if kind == "sum":
        tiles = len(outs)
        for i in range(tiles):
            outs[i][...] = total[i * (size // tiles) : (i + 1) * (size // tiles)]
    if kind == "before":
        tiles = len(outs) + 1
        for i in range(1, tiles):
            outs[i - 1][...] = value[i * (size // tiles) : (i + 1) * (size // tiles)]
    if kind in ("sketch", "probe"):
        tiles = len(extra)
        for i in range(tiles):
            outs.pop(0)[...] = value[i * (size // tiles) : (i + 1) * (size // tiles)]
    if kind == "sketch":
        sketched = total.astype(jnp.bfloat16)
        piece = None
        for i, omega in enumerate(extra):
            term = jnp.dot(
                omega[...],
                sketched[i * (size // tiles) : (i + 1) * (size // tiles)],
                preferred_element_type=jnp.float32,
            )
            piece = term if piece is None else piece + term
        keep, send = outs
        high = keep.shape[1]
        for q in range(keep.shape[0]):
            low = piece[2 * q * high : (2 * q + 1) * high]
            top = piece[(2 * q + 1) * high : (2 * q + 2) * high]
            odd = info[0] % 2 == 1
            keep[q] = jnp.where(odd, top, low)
            send[q] = jnp.where(odd, low, top).astype(jnp.bfloat16)
    if kind == "probe":
        signs = jnp.concatenate([ref[...] for ref in extra]).astype(jnp.float32)
        outs[0][...] = jnp.sum(signs * total, axis=0, keepdims=True)


def advance(step, width, kind, info, coef, band, groups, lanes, outs):
    flat = [x for group in groups for x in group]
    rows, depth = band[1].shape
    return pl.pallas_call(
        functools.partial(step_kernel, step, width, [len(group) for group in groups], lanes, kind),
        out_shape=outs,
        in_specs=[SCALAR] * 2 + [WHOLE] * (3 + len(flat)),
        out_specs=[WHOLE] * len(outs),
        compiler_params=PARAMS,
        cost_estimate=cost(6 * rows * depth, 6 * rows * depth * width),
    )(info, coef, band[1], band[0], band[2], *flat)


def fold_kernel(hop, place, keep, got, kept, send):
    odd = (place[0] // hop) % 2 == 1
    for q in range(kept.shape[0]):
        low = keep[2 * q] + got[2 * q].astype(jnp.float32)
        top = keep[2 * q + 1] + got[2 * q + 1].astype(jnp.float32)
        kept[q] = jnp.where(odd, top, low)
        send[q] = jnp.where(odd, low, top).astype(jnp.bfloat16)


def mix_kernel(send, *refs):
    terms, (quad, out) = (refs[:-2], refs[-2:])
    rows = send.shape[1]
    total = terms[0][...]
    for term in terms[1:]:
        total = total + term[...]
    quad[...] = total
    high = total.astype(jnp.bfloat16)
    low = (total - high.astype(jnp.float32)).astype(jnp.bfloat16)
    spare = out.shape[0] - rows - 2
    pad = jnp.zeros((spare, total.shape[1]), jnp.float32)
    tail = jnp.concatenate([high.astype(jnp.float32), low.astype(jnp.float32), pad])
    out[:rows] = send[0]
    out[rows:] = tail.astype(jnp.bfloat16)


def finish_kernel(scale, me, keep, got, quad, *outs):
    rows = keep.shape[1]
    count = len(outs)
    share = rows // count
    tail = got[rows:].astype(jnp.float32)
    total = (quad[...] + tail[0:1] + tail[1:2]) * scale
    spare = jnp.zeros((outs[0].shape[0] - share - 1, total.shape[1]), jnp.float32)
    gram = (keep[0] + got[:rows].astype(jnp.float32)) * scale
    for i in range(count):
        picked = gram[:share]
        for b in range(1, count):
            here = (me[0] + i) % count == b
            picked = jnp.where(here, gram[b * share : (b + 1) * share], picked)
        outs[i][:share] = picked
        outs[i][share:] = jnp.concatenate([total, spare])


def place_kernel(me, *refs):
    parts, (gram, quad) = (refs[:-2], refs[-2:])
    count = len(parts)
    share, columns = gram.shape
    width = columns // count
    for b in range(count):
        value = parts[0][...]
        for i in range(1, count):
            value = jnp.where((me[0] - i + count) % count == b, parts[i][...], value)
        gram[:, b * width : (b + 1) * width] = value[:share]
        quad[:, b * width : (b + 1) * width] = value[share : share + 1]


def small(kernel, scalars, arrays, outs):
    return pl.pallas_call(
        kernel,
        out_shape=outs,
        in_specs=[SCALAR] * len(scalars) + [WHOLE] * len(arrays),
        out_specs=[WHOLE] * len(outs),
        compiler_params=PARAMS,
        cost_estimate=cost(sum(4 * x.size for x in arrays)),
    )(*scalars, *arrays)


def program(blocks, pattern, current, previous, accum, coefs, sketch, signs):
    cells, tiles, orbs, wide = blocks.shape
    halves, local_cols = current.shape[3:]
    reach = wide // orbs // 6
    xs, me = (lax.axis_size("xsec"), lax.axis_index("xsec").astype(jnp.int32))
    wires, place = (lax.axis_size("wire"), lax.axis_index("wire").astype(jnp.int32))
    cores, core = (lax.axis_size("cols"), lax.axis_index("cols").astype(jnp.int32))
    width = local_cols // xs
    rows = cells * orbs
    others = range(1, xs)
    assert tiles == 1 and cells == reach and wires % 2 == 0 and cells % cores == 0
    assert halves == 2 and STEPS == 4

    def column_block(x, i):
        return lax.dynamic_slice_in_dim(x, (me - i) % xs * width, width, axis=x.ndim - 1)

    by_half = [current[:, 0, :, h].reshape(rows, local_cols) for h in range(halves)]
    dealt = [
        jnp.concatenate([column_block(v, i) for v in by_half], axis=1) for i in range(xs)
    ]
    fields = stacked([dealt[0]] + [from_tile(dealt[i], i) for i in others], width)

    blocks = blocks[:, 0]
    pattern = pattern[:, 0]
    mine = packed(blocks, pattern, core[None], me[None], cores, min(xs, 3))
    shares = [from_tile(mine, i) for i in others]

    even = (1 - place % 2)[None]
    band = ()
    for i in range(xs):
        parts, slot, pieces = ([blocks], jnp.zeros((1,), jnp.int32), 1)
        if i > 0:
            parts = [shares[i - 1]]
            parts += [from_tile(shares[i - 1], k, "cols") for k in range(1, cores)]
            slot, pieces = (core[None], cores)
        gap = (me + lax.iota(jnp.int32, xs)) % xs - (me + i) % xs + 1
        sizes = (cells, orbs, reach, xs, pieces)
        band = band_rows(i, parts, pattern, gap, even, slot, sizes, band)

    dealt = deal(previous, me[None])
    older = [dealt[0]] + [from_tile(dealt[i], i) for i in others]
    dealt = deal(accum, me[None])
    sums = [dealt[0]] + [from_tile(dealt[i], i) for i in others]
    ranks = sketch.shape[3]
    turned, *signed = small(
        rest_kernel, [me[None]], [sketch, signs],
        [bf16(ranks, rows)] + [bf16(rows, width)] * xs,
    )
    omega = [turned] + [from_tile(turned, i) for i in others]
    signed = [signed[0]] + [from_tile(signed[i], i) for i in others]

    full = bf16(xs * rows, width)
    piece = bf16(rows, width)
    info = place[None]

    fields = list(fields)

    def run(step, kind, field, near, far, older, sums, extra, lanes, outs):
        return advance(
            step, width, kind, info, coefs, band,
            (field, near, far, older, sums, extra), lanes, outs,
        )

    olders, totals = ([None] * halves, [None] * halves)
    zero = (0,)
    for h in range(halves):
        lane = (h * width,)
        near, far = around(fields[h])
        (nxt,) = run(
            0, "plain", [fields[h]], [near], [far], older, [], [],
            (zero, zero, zero, lane, ()), [full],
        )
        olders[h], fields[h] = (fields[h], nxt)
    for h in range(halves):
        lane = (h * width,)
        near, far = around(fields[h])
        nxt, *totals[h] = run(
            1, "sum", [fields[h]], [near], [far], [olders[h]], sums, [],
            (zero, zero, zero, zero, lane), [full] + [f32(rows, width)] * xs,
        )
        olders[h], fields[h] = (fields[h], nxt)
    befores = [None] * halves
    for h in range(halves):
        near, far = around(fields[h])
        nxt, *befores[h] = run(
            2, "before", [fields[h]], [near], [far], [olders[h]], [], [],
            (zero, zero, zero, zero, ()), [full] + [piece] * (xs - 1),
        )
        olders[h], fields[h] = (fields[h], nxt)
    newest, extras = ([None] * halves, [None] * halves)
    part = (wires // 2, ranks // wires, width)
    ends = [("sketch", omega, [f32(*part), bf16(*part)]), ("probe", signed, [f32(1, width)])]
    for h in range(halves):
        near, far = around(fields[h])
        kind, extra, outs = ends[h]
        results = run(
            3, kind, [fields[h]], [near], [far], [olders[h]], totals[h], extra,
            (zero, zero, zero, zero, zero), [piece] * xs + outs,
        )
        newest[h], extras[h] = (results[:xs], results[xs:])
    (keep, send), (quad,) = extras

    hop = 1
    high = ranks // wires
    terms = [quad]
    while 2 * hop < wires:
        got = swap_bits(send, hop)
        terms = [sum(terms[1:], terms[0])]
        terms.append(swap_bits(terms[0], hop))
        hop *= 2
        part = (wires // hop // 2, high, width)
        keep, send = small(
            functools.partial(fold_kernel, hop), [info], [keep, got],
            [f32(*part), bf16(*part)],
        )
    quad, mixed = small(mix_kernel, [], [send, *terms], [f32(1, width), bf16(high + 16, width)])
    mixed = swap_bits(mixed, hop)
    scale = 1.0 / float(rows * wires * tiles * xs) ** 0.5
    finished = small(
        functools.partial(finish_kernel, scale), [me[None]], [keep, mixed, quad],
        [f32(high // xs + 8, width)] * xs,
    )
    finished = [finished[0]] + [to_tile(finished[i], i) for i in others]
    gram, quadratic = small(
        place_kernel, [me[None]], finished, [f32(high // xs, local_cols), f32(1, local_cols)]
    )
    quadratic = quadratic[0]

    sums_back = [[totals[h][0]] + [to_tile(totals[h][i], i) for i in others] for h in range(halves)]
    before_back = [
        [fields[h]] + [to_tile(befores[h][i - 1], i) for i in others]
        for h in range(halves)
    ]
    newest_back = [
        [newest[h][0]] + [to_tile(newest[h][i], i) for i in others]
        for h in range(halves)
    ]
    shape = current.shape
    before = pl.pallas_call(
        functools.partial(before_kernel, xs),
        out_shape=bf16(*shape),
        in_specs=[SCALAR] + [WHOLE] * (halves * xs),
        out_specs=WHOLE,
        compiler_params=PARAMS,
        cost_estimate=cost(4 * current.size),
    )(me[None], *before_back[0], *before_back[1])
    flat = [x for h in range(halves) for x in newest_back[h] + before_back[h] + sums_back[h]]
    last, total = pl.pallas_call(
        functools.partial(last_kernel, xs),
        out_shape=[bf16(*shape), f32(*shape)],
        in_specs=[SCALAR, SCALAR] + [WHOLE] * len(flat),
        out_specs=[WHOLE, WHOLE],
        compiler_params=PARAMS,
        cost_estimate=cost(16 * current.size),
    )(me[None], coefs, *flat)
    return (last, before, total, gram, quadratic)


def solution(mesh):
    return jax.shard_map(
        program,
        mesh=mesh,
        in_specs=(
            P(("sample", "wire"), "xsec", None, None),
            P(("sample", "wire"), "xsec", None),
            P(("sample", "wire"), "xsec", None, None, "cols"),
            P(("sample", "wire"), "xsec", None, None, "cols"),
            P(("sample", "wire"), "xsec", None, None, "cols"),
            P(),
            P(("sample", "wire"), "xsec", None, None),
            P(("sample", "wire"), "xsec", None, "cols"),
        ),
        out_specs=(
            P(("sample", "wire"), "xsec", None, None, "cols"),
            P(("sample", "wire"), "xsec", None, None, "cols"),
            P(("sample", "wire"), "xsec", None, None, "cols"),
            P(("sample", "wire", "xsec"), "cols"),
            P(("sample", "cols")),
        ),
        check_vma=False,
    )
```

```python
import functools

import jax
import jax.numpy as jnp
from jax import lax
from jax.experimental import pallas as pl
from jax.experimental.pallas import tpu as pltpu
from jax.sharding import PartitionSpec as P

STEPS = 4
VMEM = 12 << 20
SCALAR = pl.BlockSpec(memory_space=pltpu.SMEM)
WHOLE = pl.BlockSpec(memory_space=pltpu.VMEM)
PARAMS = pltpu.CompilerParams(vmem_limit_bytes=VMEM)


def bf16(*shape):
    return jax.ShapeDtypeStruct(shape, jnp.bfloat16)


def f32(*shape):
    return jax.ShapeDtypeStruct(shape, jnp.float32)


def cost(moved, flops=0):
    return pl.CostEstimate(flops=flops, transcendentals=0, bytes_accessed=moved)


def from_tile(x, offset, axis="xsec"):
    size = lax.axis_size(axis)
    return lax.ppermute(x, axis, [((i + offset) % size, i) for i in range(size)])


def to_tile(x, offset):
    return from_tile(x, lax.axis_size("xsec") - offset)


def around(x):
    size = lax.axis_size("wire")
    first, second = ([], [])
    for i in range(0, size, 2):
        j, k = (i + 1, (i + 2) % size)
        first += [(i, j), (j, i)]
        second += [(j, k), (k, j)]
    one = lax.ppermute(x, "wire", first)
    two = lax.ppermute(x, "wire", second)
    return one, two


def swap_bits(x, hop):
    return lax.ppermute(x, "wire", [(i, i ^ hop) for i in range(lax.axis_size("wire"))])


def own_block(me, value, offset, count):
    width = value.shape[1] // count
    picked = value[:, :width]
    for b in range(1, count):
        block = value[:, b * width : (b + 1) * width]
        picked = jnp.where((me[0] - offset + count) % count == b, block, picked)
    return picked


def half_of(x, h):
    cells, _, orbs, _, columns = x.shape
    return x[...].astype(jnp.float32)[:, 0, :, h, :].reshape(cells * orbs, columns)


def deal_kernel(offsets, count, me, x, *outs):
    width = x.shape[4] // count
    for h in range(x.shape[3]):
        value = half_of(x, h)
        for offset, out in zip(offsets, outs):
            picked = own_block(me, value, offset, count)
            out[:, h * width : (h + 1) * width] = picked.astype(x.dtype)


def deal(x, me, offsets):
    count = lax.axis_size("xsec")
    cells, _, orbs, halves, columns = x.shape
    shape = (cells * orbs, halves * columns // count)
    return small(
        functools.partial(deal_kernel, offsets, count),
        [me],
        [x],
        [jax.ShapeDtypeStruct(shape, x.dtype)] * len(offsets),
    )


def stack_kernel(count, me, current, *refs):
    got, outs = (refs[: count - 1], refs[count - 1 :])
    width = outs[0].shape[1]
    rows = outs[0].shape[0] // count
    for h, out in enumerate(outs):
        out[:rows] = own_block(me, half_of(current, h), 0, count).astype(out.dtype)
        for i, ref in enumerate(got):
            out[(i + 1) * rows : (i + 2) * rows] = ref[:, h * width : (h + 1) * width]


def rest_kernel(me, sketch, signs, turned, own, *outs):
    cells, _, orbs, ranks = sketch.shape
    count = len(outs) + 1
    rows = cells * orbs
    width = own.shape[1]
    flipped = sketch[...].reshape(rows, ranks).astype(jnp.float32).T.astype(jnp.bfloat16)
    turned[...] = flipped
    value = (2 * signs[...] - 1).astype(jnp.float32).reshape(rows, signs.shape[3])
    own[...] = own_block(me, value, 0, count).astype(jnp.bfloat16)
    for i, out in enumerate(outs):
        out[:ranks] = flipped
        picked = own_block(me, value, i + 1, count).astype(jnp.bfloat16)
        for j in range(rows // width):
            out[ranks:, j * width : (j + 1) * width] = picked[j * width : (j + 1) * width]


def joined(me, refs, lanes, h, b, rows, width):
    value = None
    for i in range(len(lanes)):
        ref, lane = (refs[lanes[i][h][0]], lanes[i][h][1])
        part = ref[:rows, lane : lane + width].astype(jnp.float32)
        here = (me[0] - i + len(lanes)) % len(lanes) == b
        value = part if value is None else jnp.where(here, part, value)
    return value


def before_kernel(lanes, me, *refs):
    out = refs[-1]
    cells, _, orbs, halves, columns = out.shape
    width = columns // len(lanes)
    for h in range(halves):
        for b in range(len(lanes)):
            value = joined(me, refs, lanes, h, b, cells * orbs, width).astype(out.dtype)
            out[:, 0, :, h, b * width : (b + 1) * width] = value.reshape(cells, orbs, width)


def last_kernel(late_lanes, mid_lanes, sum_lanes, start_lanes, me, coef, *refs):
    newest, summed = refs[-2:]
    cells, _, orbs, halves, columns = newest.shape
    count = len(late_lanes)
    width = columns // count
    for h in range(halves):
        for b in range(count):
            late, mid, total, start = [
                joined(me, refs, lanes, h, b, cells * orbs, width)
                for lanes in (late_lanes, mid_lanes, sum_lanes, start_lanes)
            ]
            at = slice(b * width, (b + 1) * width)
            shape = (cells, orbs, width)
            newest[:, 0, :, h, at] = late.astype(newest.dtype).reshape(shape)
            total = start + total + coef[STEPS - 2] * mid
            total = total + coef[STEPS - 1] * late
            summed[:, 0, :, h, at] = total.reshape(shape)


def pack_kernel(core, me, pattern, blocks, out):
    share, orbs, wide = blocks.shape
    span = wide // orbs // 3
    slots = out.shape[2] // orbs // span
    zero = jnp.zeros((orbs, orbs), jnp.bfloat16)
    for c in range(share):
        cell = core[0] * share + c

        def block(d, e):
            column = 3 * d + e
            value = blocks[c, :, column * orbs : (column + 1) * orbs]
            return jnp.where(pattern[cell, column] != 0, value, zero)

        for d in range(span):
            values = [block(d, e) for e in range(3)]
            if slots == 2:
                values = [values[1], jnp.where(me[0] == 0, values[2], values[0])]
            for n, value in enumerate(values):
                at = (slots * d + n) * orbs
                out[c, :, at : at + orbs] = value


def packed(blocks, pattern, core, me, cores, slots):
    cells, orbs, wide = blocks.shape
    share = cells // cores
    shape = (share, orbs, wide // 3 * slots)
    return pl.pallas_call(
        pack_kernel,
        out_shape=bf16(*shape),
        grid_spec=pltpu.PrefetchScalarGridSpec(
            num_scalar_prefetch=3,
            grid=(1,),
            in_specs=[pl.BlockSpec((share, orbs, wide), lambda i, core, me, p: (core[0], 0, 0))],
            out_specs=pl.BlockSpec(shape, lambda i, core, me, p: (0, 0, 0)),
        ),
        compiler_params=PARAMS,
        cost_estimate=cost(4 * share * orbs * wide),
    )(core, me, pattern, blocks)


def band_kernel(tile, sizes, me, place, slot, pattern, *refs):
    cells, orbs, reach, tiles, pieces = sizes
    first, own, second = refs[-3:]
    share = cells // pieces
    span = 2 * reach + 1
    zero = jnp.zeros((orbs, orbs), jnp.bfloat16)
    slots = refs[0].shape[2] // orbs // span
    masked = tile == 0

    def write(parts):
        def block(c, u, x):
            d = x - c
            if d < 0 or d >= span:
                return zero
            ref = parts[c // share]

            def at(e):
                column = slots * d + e
                value = ref[c % share, :, column * orbs : (column + 1) * orbs]
                if masked:
                    value = jnp.where(pattern[c, column] != 0, value, zero)
                return value

            if slots == 2:
                return at(0 if u == tile else 1)
            if u == tile:
                return at(1)
            gap = lax.rem(me[0] + u, tiles) - lax.rem(me[0] + tile, tiles) + 1
            return jnp.where(gap == 0, at(0), jnp.where(gap == 2, at(2), zero))

        turn = lax.rem(place[0], 2) == 0
        for c in range(cells):
            rows = slice(c * orbs, (c + 1) * orbs)
            for u in range(tiles):
                for j in range(cells):
                    at = (u * cells + j) * orbs
                    own[rows, at : at + orbs] = block(c, u, reach + j)
                for j in range(reach):
                    at = (u * reach + j) * orbs
                    left, right = (block(c, u, j), block(c, u, reach + cells + j))
                    first[rows, at : at + orbs] = jnp.where(turn, right, left)
                    second[rows, at : at + orbs] = jnp.where(turn, left, right)

    if pieces == 1:
        write(refs[:1])
        return
    for k in range(pieces):

        @pl.when(slot[0] == k)
        def _():
            write([refs[(piece - k) % pieces] for piece in range(pieces)])


def band_rows(tile, parts, pattern, me, place, slot, sizes, held):
    cells, orbs, reach, tiles, _ = sizes
    rows = cells * orbs
    shapes = [(tiles * rows, tiles * n * orbs) for n in (reach, cells, reach)]
    n_in = 4 + len(parts)
    return pl.pallas_call(
        functools.partial(band_kernel, tile, sizes),
        out_shape=[bf16(*s) for s in shapes],
        grid=(1,),
        in_specs=[SCALAR] * 4
        + [pl.BlockSpec(p.shape, lambda i: (0, 0, 0)) for p in parts]
        + [pl.BlockSpec(memory_space=pl.ANY)] * len(held),
        out_specs=[pl.BlockSpec((rows, s[1]), lambda i: (tile, 0)) for s in shapes],
        input_output_aliases={n_in + i: i for i in range(len(held))},
        compiler_params=PARAMS,
        cost_estimate=cost(4 * rows * tiles * 3 * cells * orbs),
    )(me, place, slot, pattern, *parts, *held)


def step_kernel(step, tiles, width, counts, lanes, kind, *refs):
    refs = list(refs)

    def take(n):
        taken = refs[:n]
        del refs[:n]
        return taken

    place = take(1)[0] if kind == "sketch" else None
    coef = take(1)[0] if kind in ("sum", "sketch", "probe") else None
    own, first, second = take(3)
    field, near, far, older, sums, start, extra = [take(n) for n in counts]
    outs = refs

    def parts(group, lane):
        return [ref[:, low : low + width] for ref, low in zip(group, lane)]

    image = None
    for band, group in zip((own, first, second), (field, near, far)):
        at = 0
        for ref in group:
            depth = ref.shape[0]
            term = jnp.dot(
                band[:, at : at + depth], ref[...], preferred_element_type=jnp.float32
            )
            image = term if image is None else image + term
            at += depth

    old = jnp.concatenate(parts(older, lanes[0])).astype(jnp.float32)
    value = (2.0 * image - old).astype(jnp.bfloat16)
    rows = value.shape[0] // tiles

    if kind in ("plain", "sum", "before"):
        outs.pop(0)[...] = value
    if kind in ("sum", "sketch", "probe"):
        now = jnp.concatenate([ref[...] for ref in field]).astype(jnp.float32)
        total = coef[step - 1] * now + coef[step] * value.astype(jnp.float32)
        if sums:
            total = jnp.concatenate(parts(start, lanes[2])) + jnp.concatenate(parts(sums, lanes[1])) + total
    if kind == "sum":
        for i, out in enumerate(outs):
            mine = total[i * rows : (i + 1) * rows]
            if out.shape[1] == width:
                out[...] = mine
            else:
                out[:, :width] = extra[i - 1][...]
                out[:, width:] = mine
    if kind == "before":
        for i, out in enumerate(outs):
            at = slice((i + 1) * rows, (i + 2) * rows)
            out[:, :width] = extra[0][at]
            out[:, width:] = value[at]
    if kind in ("sketch", "probe"):
        for i in range(len(extra)):
            outs.pop(0)[...] = value[i * rows : (i + 1) * rows]
    if kind == "sketch":
        sketched = total.astype(jnp.bfloat16)
        keep, send = outs
        high = keep.shape[1]
        ranks = 2 * keep.shape[0] * high
        piece = None
        for i, omega in enumerate(extra):
            term = jnp.dot(
                omega[:ranks],
                sketched[i * rows : (i + 1) * rows],
                preferred_element_type=jnp.float32,
            )
            piece = term if piece is None else piece + term
        odd = place[0] % 2 == 1
        for q in range(keep.shape[0]):
            low = piece[2 * q * high : (2 * q + 1) * high]
            top = piece[(2 * q + 1) * high : (2 * q + 2) * high]
            keep[q] = jnp.where(odd, top, low)
            send[q] = jnp.where(odd, low, top).astype(jnp.bfloat16)
    if kind == "probe":
        signs = [extra[0][...]]
        for ref in extra[1:]:
            ranks = ref.shape[0] - width
            signs += [ref[ranks:, j * width : (j + 1) * width] for j in range(rows // width)]
        signs = jnp.concatenate(signs).astype(jnp.float32)
        outs[0][...] = jnp.sum(signs * total, axis=0, keepdims=True)


def advance(step, width, kind, scalars, band, groups, lanes, outs):
    tiles = lax.axis_size("xsec")
    flat = [x for group in groups for x in group]
    rows, depth = band[1].shape
    return pl.pallas_call(
        functools.partial(
            step_kernel, step, tiles, width, [len(group) for group in groups], lanes, kind
        ),
        out_shape=outs,
        in_specs=[SCALAR] * len(scalars) + [WHOLE] * (3 + len(flat)),
        out_specs=[WHOLE] * len(outs),
        compiler_params=PARAMS,
        cost_estimate=cost(6 * rows * depth, 6 * rows * depth * width),
    )(*scalars, band[1], band[0], band[2], *flat)


def fold_kernel(hop, place, keep, got, kept, send):
    odd = (place[0] // hop) % 2 == 1
    for q in range(kept.shape[0]):
        low = keep[2 * q] + got[2 * q].astype(jnp.float32)
        top = keep[2 * q + 1] + got[2 * q + 1].astype(jnp.float32)
        kept[q] = jnp.where(odd, top, low)
        send[q] = jnp.where(odd, low, top).astype(jnp.bfloat16)


def mix_kernel(send, *refs):
    terms, (quad, out) = (refs[:-2], refs[-2:])
    rows = send.shape[1]
    total = terms[0][...]
    for term in terms[1:]:
        total = total + term[...]
    quad[...] = total
    high = total.astype(jnp.bfloat16)
    low = (total - high.astype(jnp.float32)).astype(jnp.bfloat16)
    spare = out.shape[0] - rows - 2
    pad = jnp.zeros((spare, total.shape[1]), jnp.float32)
    tail = jnp.concatenate([high.astype(jnp.float32), low.astype(jnp.float32), pad])
    out[:rows] = send[0]
    out[rows:] = tail.astype(jnp.bfloat16)


def finish_kernel(scale, me, keep, got, quad, *outs):
    rows = keep.shape[1]
    count = len(outs)
    share = rows // count
    tail = got[rows:].astype(jnp.float32)
    total = (quad[...] + tail[0:1] + tail[1:2]) * scale
    spare = jnp.zeros((outs[0].shape[0] - share - 1, total.shape[1]), jnp.float32)
    gram = (keep[0] + got[:rows].astype(jnp.float32)) * scale
    for i in range(count):
        picked = gram[:share]
        for b in range(1, count):
            here = (me[0] + i) % count == b
            picked = jnp.where(here, gram[b * share : (b + 1) * share], picked)
        outs[i][:share] = picked
        outs[i][share:] = jnp.concatenate([total, spare])


def place_kernel(me, *refs):
    parts, (gram, quad) = (refs[:-2], refs[-2:])
    count = len(parts)
    share, columns = gram.shape
    width = columns // count
    for b in range(count):
        value = parts[0][...]
        for i in range(1, count):
            value = jnp.where((me[0] - i + count) % count == b, parts[i][...], value)
        gram[:, b * width : (b + 1) * width] = value[:share]
        quad[:, b * width : (b + 1) * width] = value[share : share + 1]


def small(kernel, scalars, arrays, outs):
    return pl.pallas_call(
        kernel,
        out_shape=outs,
        in_specs=[SCALAR] * len(scalars) + [WHOLE] * len(arrays),
        out_specs=[WHOLE] * len(outs),
        compiler_params=PARAMS,
        cost_estimate=cost(sum(4 * x.size for x in arrays)),
    )(*scalars, *arrays)


def program(blocks, pattern, current, previous, accum, coefs, sketch, signs):
    cells, tiles, orbs, wide = blocks.shape
    halves, local_cols = current.shape[3:]
    reach = wide // orbs // 6
    xs, me = (lax.axis_size("xsec"), lax.axis_index("xsec").astype(jnp.int32))
    wires, place = (lax.axis_size("wire"), lax.axis_index("wire").astype(jnp.int32))
    cores, core = (lax.axis_size("cols"), lax.axis_index("cols").astype(jnp.int32))
    width = local_cols // xs
    rows = cells * orbs
    others = range(1, xs)
    assert tiles == 1 and cells == reach and wires % 2 == 0 and cells % cores == 0
    assert halves == 2 and STEPS == 4

    everyone = range(xs)
    assert rows % width == 0

    leaving = deal(current, me[None], others)
    coming = [from_tile(leaving[i - 1], i) for i in others]
    fields = small(
        functools.partial(stack_kernel, xs), [me[None]], [current, *coming],
        [bf16(xs * rows, width)] * halves,
    )

    blocks = blocks[:, 0]
    pattern = pattern[:, 0]
    mine = packed(blocks, pattern, core[None], me[None], cores, min(xs, 3))
    shares = [from_tile(mine, i) for i in others]

    band = ()
    for i in range(xs):
        parts, slot, pieces = ([blocks], core[None], 1)
        if i > 0:
            parts = [shares[i - 1]]
            parts += [from_tile(shares[i - 1], k, "cols") for k in range(1, cores)]
            slot, pieces = (core[None], cores)
        sizes = (cells, orbs, reach, xs, pieces)
        band = band_rows(i, parts, pattern, me[None], place[None], slot, sizes, band)

    dealt = deal(previous, me[None], everyone)
    older = [dealt[0]] + [from_tile(dealt[i], i) for i in others]
    dealt = deal(accum, me[None], everyone)
    starts = dealt
    accums = [dealt[0]] + [from_tile(dealt[i], i) for i in others]
    ranks = sketch.shape[3]
    turned, signed, *leaving = small(
        rest_kernel, [me[None]], [sketch, signs],
        [bf16(ranks, rows), bf16(rows, width)] + [bf16(ranks + width, rows)] * (xs - 1),
    )
    coming = [from_tile(leaving[i - 1], i) for i in others]
    omega, signed = ([turned, *coming], [signed, *coming])

    full = bf16(xs * rows, width)
    piece = bf16(rows, width)
    info = place[None]
    fields = list(fields)
    olders, totals = ([None] * halves, [None] * halves)
    zero = (0,) * xs

    def run(step, h, kind, older, sums, start, extra, lanes, outs):
        near, far = around(fields[h])
        scalars = {"sum": [coefs], "sketch": [info, coefs], "probe": [coefs]}.get(kind, [])
        return advance(
            step, width, kind, scalars, band,
            ([fields[h]], [near], [far], older, sums, start, extra), lanes, outs,
        )

    for h in range(halves):
        (nxt,) = run(0, h, "plain", older, [], [], [], ((h * width,) * xs, (), ()), [full])
        olders[h], fields[h] = (fields[h], nxt)
    for h in range(halves):
        extra = totals[0][1:] if h else []
        outs = [full, f32(rows, width)] + [f32(rows, (h + 1) * width)] * (xs - 1)
        nxt, *totals[h] = run(
            1, h, "sum", [olders[h]], [], [], extra, (zero, (), ()), outs
        )
        olders[h], fields[h] = (fields[h], nxt)
    for h in range(halves):
        kind, extra, outs = ("plain", [], [])
        if h:
            kind, extra, outs = ("before", [fields[0]], [bf16(rows, 2 * width)] * (xs - 1))
        nxt, *befores = run(2, h, kind, [olders[h]], [], [], extra, (zero, (), ()), [full] + outs)
        olders[h], fields[h] = (fields[h], nxt)
    newest, extras = ([None] * halves, [None] * halves)
    part = (wires // 2, ranks // wires, width)
    ends = [("sketch", omega, [f32(*part), bf16(*part)]), ("probe", signed, [f32(1, width)])]
    for h in range(halves):
        kind, extra, outs = ends[h]
        lanes = (zero, (0,) + (h * width,) * (xs - 1), (h * width,) * xs)
        results = run(
            3, h, kind, [olders[h]], totals[h], accums, extra, lanes, [piece] * xs + outs
        )
        newest[h], extras[h] = (results[:xs], results[xs:])
    (keep, send), (quad,) = extras

    hop = 1
    high = ranks // wires
    terms = [quad]
    while 2 * hop < wires:
        got = swap_bits(send, hop)
        terms = [sum(terms[1:], terms[0])]
        terms.append(swap_bits(terms[0], hop))
        hop *= 2
        part = (wires // hop // 2, high, width)
        keep, send = small(
            functools.partial(fold_kernel, hop), [info], [keep, got],
            [f32(*part), bf16(*part)],
        )
    quad, mixed = small(mix_kernel, [], [send, *terms], [f32(1, width), bf16(high + 16, width)])
    mixed = swap_bits(mixed, hop)
    scale = 1.0 / float(rows * wires * tiles * xs) ** 0.5
    finished = small(
        functools.partial(finish_kernel, scale), [me[None]], [keep, mixed, quad],
        [f32(high // xs + 8, width)] * xs,
    )
    finished = [finished[0]] + [to_tile(finished[i], i) for i in others]
    gram, quadratic = small(
        place_kernel, [me[None]], finished, [f32(high // xs, local_cols), f32(1, local_cols)]
    )
    quadratic = quadratic[0]

    sums_back = [totals[0][0], totals[1][0]]
    sums_back += [to_tile(totals[1][i], i) for i in others]
    before_back = [fields[0], fields[1]]
    before_back += [to_tile(befores[i - 1], i) for i in others]
    newest_back = [newest[0][0], newest[1][0]]
    for i in others:
        newest_back += [to_tile(newest[h][i], i) for h in range(halves)]

    def paired(start):
        return [[(start, 0), (start + 1, 0)]] + [
            [(start + 1 + i, 0), (start + 1 + i, width)] for i in others
        ]

    shape = current.shape
    (before,) = small(
        functools.partial(before_kernel, paired(0)), [me[None]], before_back,
        [bf16(*shape)],
    )
    late = [[(2 * i, 0), (2 * i + 1, 0)] for i in everyone]
    arrays, lanes = (list(newest_back), [late])
    for group in (before_back, sums_back):
        lanes.append(paired(len(arrays)))
        arrays += group
    lanes.append([[(len(arrays) + i, h * width) for h in range(halves)] for i in everyone])
    arrays += starts
    last, total = small(
        functools.partial(last_kernel, *lanes), [me[None], coefs], arrays,
        [bf16(*shape), f32(*shape)],
    )
    return (last, before, total, gram, quadratic)


def solution(mesh):
    return jax.shard_map(
        program,
        mesh=mesh,
        in_specs=(
            P(("sample", "wire"), "xsec", None, None),
            P(("sample", "wire"), "xsec", None),
            P(("sample", "wire"), "xsec", None, None, "cols"),
            P(("sample", "wire"), "xsec", None, None, "cols"),
            P(("sample", "wire"), "xsec", None, None, "cols"),
            P(),
            P(("sample", "wire"), "xsec", None, None),
            P(("sample", "wire"), "xsec", None, "cols"),
        ),
        out_specs=(
            P(("sample", "wire"), "xsec", None, None, "cols"),
            P(("sample", "wire"), "xsec", None, None, "cols"),
            P(("sample", "wire"), "xsec", None, None, "cols"),
            P(("sample", "wire", "xsec"), "cols"),
            P(("sample", "cols")),
        ),
        check_vma=False,
    )
```

```python
import functools

import jax
import jax.numpy as jnp
from jax import lax
from jax.experimental import pallas as pl
from jax.experimental.pallas import tpu as pltpu
from jax.sharding import PartitionSpec as P

STEPS = 4
VMEM = 12 << 20
SCALAR = pl.BlockSpec(memory_space=pltpu.SMEM)
WHOLE = pl.BlockSpec(memory_space=pltpu.VMEM)
PARAMS = pltpu.CompilerParams(vmem_limit_bytes=VMEM)


def bf16(*shape):
    return jax.ShapeDtypeStruct(shape, jnp.bfloat16)


def f32(*shape):
    return jax.ShapeDtypeStruct(shape, jnp.float32)


def cost(moved, flops=0):
    return pl.CostEstimate(flops=flops, transcendentals=0, bytes_accessed=moved)


def from_tile(x, offset, axis="xsec"):
    size = lax.axis_size(axis)
    return lax.ppermute(x, axis, [((i + offset) % size, i) for i in range(size)])


def to_tile(x, offset):
    return from_tile(x, lax.axis_size("xsec") - offset)


def around(x):
    size = lax.axis_size("wire")
    first, second = ([], [])
    for i in range(0, size, 2):
        j, k = (i + 1, (i + 2) % size)
        first += [(i, j), (j, i)]
        second += [(j, k), (k, j)]
    one = lax.ppermute(x, "wire", first)
    two = lax.ppermute(x, "wire", second)
    return one, two


def swap_bits(x, hop):
    return lax.ppermute(x, "wire", [(i, i ^ hop) for i in range(lax.axis_size("wire"))])


def own_block(me, value, offset, count):
    width = value.shape[1] // count
    picked = value[:, :width]
    for b in range(1, count):
        block = value[:, b * width : (b + 1) * width]
        picked = jnp.where((me[0] - offset + count) % count == b, block, picked)
    return picked


def half_of(x, h):
    cells, _, orbs, _, columns = x.shape
    return x[...].astype(jnp.float32)[:, 0, :, h, :].reshape(cells * orbs, columns)


def deal_kernel(offsets, count, me, x, *outs):
    width = x.shape[4] // count
    for h in range(x.shape[3]):
        value = half_of(x, h)
        for offset, out in zip(offsets, outs):
            picked = own_block(me, value, offset, count)
            out[:, h * width : (h + 1) * width] = picked.astype(x.dtype)


def deal(x, me, offsets):
    count = lax.axis_size("xsec")
    cells, _, orbs, halves, columns = x.shape
    shape = (cells * orbs, halves * columns // count)
    return small(
        functools.partial(deal_kernel, offsets, count),
        [me],
        [x],
        [jax.ShapeDtypeStruct(shape, x.dtype)] * len(offsets),
    )


def stack_kernel(*refs):
    count = len(refs) - 2
    width = refs[-1].shape[1]
    rows = refs[0].shape[0]
    for h, out in enumerate(refs[count:]):
        for i, ref in enumerate(refs[:count]):
            out[i * rows : (i + 1) * rows] = ref[:, h * width : (h + 1) * width]


def rest_kernel(me, sketch, signs, turned, own, *outs):
    cells, _, orbs, ranks = sketch.shape
    count = len(outs) + 1
    rows = cells * orbs
    width = own.shape[1]
    flipped = sketch[...].reshape(rows, ranks).astype(jnp.float32).T.astype(jnp.bfloat16)
    turned[...] = flipped
    value = (2 * signs[...] - 1).astype(jnp.float32).reshape(rows, signs.shape[3])
    own[...] = own_block(me, value, 0, count).astype(jnp.bfloat16)
    for i, out in enumerate(outs):
        out[:ranks] = flipped
        picked = own_block(me, value, i + 1, count).astype(jnp.bfloat16)
        for j in range(rows // width):
            out[ranks:, j * width : (j + 1) * width] = picked[j * width : (j + 1) * width]


def joined(me, refs, lanes, h, b, rows, width):
    value = None
    for i in range(len(lanes)):
        ref, lane = (refs[lanes[i][h][0]], lanes[i][h][1])
        part = ref[:rows, lane : lane + width].astype(jnp.float32)
        here = (me[0] - i + len(lanes)) % len(lanes) == b
        value = part if value is None else jnp.where(here, part, value)
    return value


def before_kernel(lanes, me, *refs):
    out = refs[-1]
    cells, _, orbs, halves, columns = out.shape
    width = columns // len(lanes)
    for h in range(halves):
        for b in range(len(lanes)):
            value = joined(me, refs, lanes, h, b, cells * orbs, width).astype(out.dtype)
            out[:, 0, :, h, b * width : (b + 1) * width] = value.reshape(cells, orbs, width)


def last_kernel(late_lanes, mid_lanes, sum_lanes, start_lanes, me, coef, *refs):
    newest, summed = refs[-2:]
    cells, _, orbs, halves, columns = newest.shape
    count = len(late_lanes)
    width = columns // count
    for h in range(halves):
        for b in range(count):
            late, mid, total, start = [
                joined(me, refs, lanes, h, b, cells * orbs, width)
                for lanes in (late_lanes, mid_lanes, sum_lanes, start_lanes)
            ]
            at = slice(b * width, (b + 1) * width)
            shape = (cells, orbs, width)
            newest[:, 0, :, h, at] = late.astype(newest.dtype).reshape(shape)
            total = start + total + coef[:, STEPS - 2 : STEPS - 1] * mid
            total = total + coef[:, STEPS - 1 : STEPS] * late
            summed[:, 0, :, h, at] = total.reshape(shape)


def pack_kernel(core, me, pattern, blocks, out):
    share, orbs, wide = blocks.shape
    span = wide // orbs // 3
    slots = out.shape[2] // orbs // span
    zero = jnp.zeros((orbs, orbs), jnp.bfloat16)
    for c in range(share):
        cell = core[0] * share + c

        def block(d, e):
            column = 3 * d + e
            value = blocks[c, :, column * orbs : (column + 1) * orbs]
            return jnp.where(pattern[cell, column] != 0, value, zero)

        for d in range(span):
            values = [block(d, e) for e in range(3)]
            if slots == 2:
                values = [values[1], jnp.where(me[0] == 0, values[2], values[0])]
            for n, value in enumerate(values):
                at = (slots * d + n) * orbs
                out[c, :, at : at + orbs] = value


def packed(blocks, pattern, core, me, cores, slots):
    cells, orbs, wide = blocks.shape
    share = cells // cores
    shape = (share, orbs, wide // 3 * slots)
    return pl.pallas_call(
        pack_kernel,
        out_shape=bf16(*shape),
        grid_spec=pltpu.PrefetchScalarGridSpec(
            num_scalar_prefetch=3,
            grid=(1,),
            in_specs=[pl.BlockSpec((share, orbs, wide), lambda i, core, me, p: (core[0], 0, 0))],
            out_specs=pl.BlockSpec(shape, lambda i, core, me, p: (0, 0, 0)),
        ),
        compiler_params=PARAMS,
        cost_estimate=cost(4 * share * orbs * wide),
    )(core, me, pattern, blocks)


def band_kernel(tile, sizes, me, place, slot, pattern, *refs):
    cells, orbs, reach, tiles, pieces = sizes
    first, own, second = refs[-3:]
    share = cells // pieces
    span = 2 * reach + 1
    zero = jnp.zeros((orbs, orbs), jnp.bfloat16)
    slots = refs[0].shape[2] // orbs // span
    masked = tile == 0

    def write(parts):
        def block(c, u, x):
            d = x - c
            if d < 0 or d >= span:
                return zero
            ref = parts[c // share]

            def at(e):
                column = slots * d + e
                value = ref[c % share, :, column * orbs : (column + 1) * orbs]
                if masked:
                    value = jnp.where(pattern[c, column] != 0, value, zero)
                return value

            if slots == 2:
                return at(0 if u == tile else 1)
            if u == tile:
                return at(1)
            gap = lax.rem(me[0] + u, tiles) - lax.rem(me[0] + tile, tiles) + 1
            return jnp.where(gap == 0, at(0), jnp.where(gap == 2, at(2), zero))

        turn = lax.rem(place[0], 2) == 0
        for c in range(cells):
            rows = slice(c * orbs, (c + 1) * orbs)
            for u in range(tiles):
                for j in range(cells):
                    at = (u * cells + j) * orbs
                    own[rows, at : at + orbs] = block(c, u, reach + j)
                for j in range(reach):
                    at = (u * reach + j) * orbs
                    left, right = (block(c, u, j), block(c, u, reach + cells + j))
                    first[rows, at : at + orbs] = jnp.where(turn, right, left)
                    second[rows, at : at + orbs] = jnp.where(turn, left, right)

    if pieces == 1:
        write(refs[:1])
        return
    for k in range(pieces):

        @pl.when(slot[0] == k)
        def _():
            write([refs[(piece - k) % pieces] for piece in range(pieces)])


def band_rows(tile, parts, pattern, me, place, slot, sizes, held):
    cells, orbs, reach, tiles, _ = sizes
    rows = cells * orbs
    shapes = [(tiles * rows, tiles * n * orbs) for n in (reach, cells, reach)]
    n_in = 4 + len(parts)
    return pl.pallas_call(
        functools.partial(band_kernel, tile, sizes),
        out_shape=[bf16(*s) for s in shapes],
        grid=(1,),
        in_specs=[SCALAR] * 4
        + [pl.BlockSpec(p.shape, lambda i: (0, 0, 0)) for p in parts]
        + [pl.BlockSpec(memory_space=pl.ANY)] * len(held),
        out_specs=[pl.BlockSpec((rows, s[1]), lambda i: (tile, 0)) for s in shapes],
        input_output_aliases={n_in + i: i for i in range(len(held))},
        compiler_params=PARAMS,
        cost_estimate=cost(4 * rows * tiles * 3 * cells * orbs),
    )(me, place, slot, pattern, *parts, *held)


def step_kernel(step, tiles, width, counts, lanes, kind, *refs):
    refs = list(refs)

    def take(n):
        taken = refs[:n]
        del refs[:n]
        return taken

    place = take(1)[0] if kind == "sketch" else None
    own, first, second = take(3)
    coef = take(1)[0] if kind in ("sum", "sketch", "probe") else None
    field, near, far, older, sums, start, extra = [take(n) for n in counts]
    outs = refs

    def parts(group, lane):
        return [ref[:, low : low + width] for ref, low in zip(group, lane)]

    image = None
    for band, group in zip((own, first, second), (field, near, far)):
        at = 0
        for ref in group:
            depth = ref.shape[0]
            term = jnp.dot(
                band[:, at : at + depth], ref[...], preferred_element_type=jnp.float32
            )
            image = term if image is None else image + term
            at += depth

    old = jnp.concatenate(parts(older, lanes[0])).astype(jnp.float32)
    value = (2.0 * image - old).astype(jnp.bfloat16)
    rows = value.shape[0] // tiles

    if kind in ("plain", "sum", "before"):
        outs.pop(0)[...] = value
    if kind in ("sum", "sketch", "probe"):
        now = jnp.concatenate([ref[...] for ref in field]).astype(jnp.float32)
        total = coef[:, step - 1 : step] * now + coef[:, step : step + 1] * value.astype(jnp.float32)
        if sums:
            total = jnp.concatenate(parts(start, lanes[2])) + jnp.concatenate(parts(sums, lanes[1])) + total
    if kind == "sum":
        for i, out in enumerate(outs):
            mine = total[i * rows : (i + 1) * rows]
            if out.shape[1] == width:
                out[...] = mine
            else:
                out[:, :width] = extra[i - 1][...]
                out[:, width:] = mine
    if kind == "before":
        for i, out in enumerate(outs):
            at = slice((i + 1) * rows, (i + 2) * rows)
            out[:, :width] = extra[0][at]
            out[:, width:] = value[at]
    if kind in ("sketch", "probe"):
        for i in range(len(extra)):
            outs.pop(0)[...] = value[i * rows : (i + 1) * rows]
    if kind == "sketch":
        sketched = total.astype(jnp.bfloat16)
        keep, send = outs
        high = keep.shape[1]
        ranks = 2 * keep.shape[0] * high
        piece = None
        for i, omega in enumerate(extra):
            term = jnp.dot(
                omega[:ranks],
                sketched[i * rows : (i + 1) * rows],
                preferred_element_type=jnp.float32,
            )
            piece = term if piece is None else piece + term
        odd = place[0] % 2 == 1
        for q in range(keep.shape[0]):
            low = piece[2 * q * high : (2 * q + 1) * high]
            top = piece[(2 * q + 1) * high : (2 * q + 2) * high]
            keep[q] = jnp.where(odd, top, low)
            send[q] = jnp.where(odd, low, top).astype(jnp.bfloat16)
    if kind == "probe":
        signs = [extra[0][...]]
        for ref in extra[1:]:
            ranks = ref.shape[0] - width
            signs += [ref[ranks:, j * width : (j + 1) * width] for j in range(rows // width)]
        signs = jnp.concatenate(signs).astype(jnp.float32)
        outs[0][...] = jnp.sum(signs * total, axis=0, keepdims=True)


def advance(step, width, kind, scalars, coefs, band, groups, lanes, outs):
    tiles = lax.axis_size("xsec")
    flat = coefs + [x for group in groups for x in group]
    rows, depth = band[1].shape
    return pl.pallas_call(
        functools.partial(
            step_kernel, step, tiles, width, [len(group) for group in groups], lanes, kind
        ),
        out_shape=outs,
        in_specs=[SCALAR] * len(scalars) + [WHOLE] * (3 + len(flat)),
        out_specs=[WHOLE] * len(outs),
        compiler_params=PARAMS,
        cost_estimate=cost(6 * rows * depth, 6 * rows * depth * width),
    )(*scalars, band[1], band[0], band[2], *flat)


def fold_kernel(hop, place, keep, got, kept, send):
    odd = (place[0] // hop) % 2 == 1
    for q in range(kept.shape[0]):
        low = keep[2 * q] + got[2 * q].astype(jnp.float32)
        top = keep[2 * q + 1] + got[2 * q + 1].astype(jnp.float32)
        kept[q] = jnp.where(odd, top, low)
        send[q] = jnp.where(odd, low, top).astype(jnp.bfloat16)


def mix_kernel(send, *refs):
    terms, (quad, out) = (refs[:-2], refs[-2:])
    rows = send.shape[1]
    total = terms[0][...]
    for term in terms[1:]:
        total = total + term[...]
    quad[...] = total
    high = total.astype(jnp.bfloat16)
    low = (total - high.astype(jnp.float32)).astype(jnp.bfloat16)
    spare = out.shape[0] - rows - 2
    pad = jnp.zeros((spare, total.shape[1]), jnp.float32)
    tail = jnp.concatenate([high.astype(jnp.float32), low.astype(jnp.float32), pad])
    out[:rows] = send[0]
    out[rows:] = tail.astype(jnp.bfloat16)


def finish_kernel(count, scale, me, keep, got, quad, *refs):
    rest, outs = (refs[:-count], refs[-count:])
    rows = keep.shape[1]
    share = rows // count
    tail = got[rows:].astype(jnp.float32)
    total = quad[...] + tail[0:1] + tail[1:2]
    for term in rest:
        total = total + term[...]
    total = total * scale
    spare = jnp.zeros((outs[0].shape[0] - share - 1, total.shape[1]), jnp.float32)
    gram = (keep[0] + got[:rows].astype(jnp.float32)) * scale
    for i in range(count):
        picked = gram[:share]
        for b in range(1, count):
            here = (me[0] + i) % count == b
            picked = jnp.where(here, gram[b * share : (b + 1) * share], picked)
        outs[i][:share] = picked
        outs[i][share:] = jnp.concatenate([total, spare])


def place_kernel(me, *refs):
    parts, (gram, quad) = (refs[:-2], refs[-2:])
    count = len(parts)
    share, columns = gram.shape
    width = columns // count
    for b in range(count):
        value = parts[0][...]
        for i in range(1, count):
            value = jnp.where((me[0] - i + count) % count == b, parts[i][...], value)
        gram[:, b * width : (b + 1) * width] = value[:share]
        quad[:, b * width : (b + 1) * width] = value[share : share + 1]


def small(kernel, scalars, arrays, outs):
    return pl.pallas_call(
        kernel,
        out_shape=outs,
        in_specs=[SCALAR] * len(scalars) + [WHOLE] * len(arrays),
        out_specs=[WHOLE] * len(outs),
        compiler_params=PARAMS,
        cost_estimate=cost(sum(4 * x.size for x in arrays)),
    )(*scalars, *arrays)


def program(blocks, pattern, current, previous, accum, coefs, sketch, signs):
    cells, tiles, orbs, wide = blocks.shape
    halves, local_cols = current.shape[3:]
    reach = wide // orbs // 6
    xs, me = (lax.axis_size("xsec"), lax.axis_index("xsec").astype(jnp.int32))
    wires, place = (lax.axis_size("wire"), lax.axis_index("wire").astype(jnp.int32))
    cores, core = (lax.axis_size("cols"), lax.axis_index("cols").astype(jnp.int32))
    width = local_cols // xs
    rows = cells * orbs
    others = range(1, xs)
    assert tiles == 1 and cells == reach and wires % 2 == 0 and cells % cores == 0
    assert halves == 2 and STEPS == 4

    everyone = range(xs)
    coefs = coefs[None]
    assert rows % width == 0

    leaving = deal(current, me[None], others)
    coming = [from_tile(leaving[i - 1], i) for i in others]
    staying = deal(current, me[None], [0])
    fields = small(stack_kernel, [], [*staying, *coming], [bf16(xs * rows, width)] * halves)

    blocks = blocks[:, 0]
    pattern = pattern[:, 0]
    mine = packed(blocks, pattern, core[None], me[None], cores, min(xs, 3))
    shares = [from_tile(mine, i) for i in others]

    band = ()
    for i in range(xs):
        parts, slot, pieces = ([blocks], core[None], 1)
        if i > 0:
            parts = [shares[i - 1]]
            parts += [from_tile(shares[i - 1], k, "cols") for k in range(1, cores)]
            slot, pieces = (core[None], cores)
        sizes = (cells, orbs, reach, xs, pieces)
        band = band_rows(i, parts, pattern, me[None], place[None], slot, sizes, band)

    dealt = deal(previous, me[None], everyone)
    older = [dealt[0]] + [from_tile(dealt[i], i) for i in others]
    dealt = deal(accum, me[None], everyone)
    starts = dealt
    accums = [dealt[0]] + [from_tile(dealt[i], i) for i in others]
    ranks = sketch.shape[3]
    turned, signed, *leaving = small(
        rest_kernel, [me[None]], [sketch, signs],
        [bf16(ranks, rows), bf16(rows, width)] + [bf16(ranks + width, rows)] * (xs - 1),
    )
    coming = [from_tile(leaving[i - 1], i) for i in others]
    omega, signed = ([turned, *coming], [signed, *coming])

    full = bf16(xs * rows, width)
    piece = bf16(rows, width)
    info = place[None]
    fields = list(fields)
    olders, totals = ([None] * halves, [None] * halves)
    zero = (0,) * xs

    def run(step, h, kind, older, sums, start, extra, lanes, outs):
        near, far = around(fields[h])
        scalars = [info] if kind == "sketch" else []
        weights = [coefs] if kind in ("sum", "sketch", "probe") else []
        return advance(
            step, width, kind, scalars, weights, band,
            ([fields[h]], [near], [far], older, sums, start, extra), lanes, outs,
        )

    for h in range(halves):
        (nxt,) = run(0, h, "plain", older, [], [], [], ((h * width,) * xs, (), ()), [full])
        olders[h], fields[h] = (fields[h], nxt)
    for h in range(halves):
        extra = totals[0][1:] if h else []
        outs = [full, f32(rows, width)] + [f32(rows, (h + 1) * width)] * (xs - 1)
        nxt, *totals[h] = run(
            1, h, "sum", [olders[h]], [], [], extra, (zero, (), ()), outs
        )
        olders[h], fields[h] = (fields[h], nxt)
    for h in range(halves):
        kind, extra, outs = ("plain", [], [])
        if h:
            kind, extra, outs = ("before", [fields[0]], [bf16(rows, 2 * width)] * (xs - 1))
        nxt, *befores = run(2, h, kind, [olders[h]], [], [], extra, (zero, (), ()), [full] + outs)
        olders[h], fields[h] = (fields[h], nxt)
    newest, extras = ([None] * halves, [None] * halves)
    part = (wires // 2, ranks // wires, width)
    ends = [("sketch", omega, [f32(*part), bf16(*part)]), ("probe", signed, [f32(1, width)])]
    for h in range(halves):
        kind, extra, outs = ends[h]
        lanes = (zero, (0,) + (h * width,) * (xs - 1), (h * width,) * xs)
        results = run(
            3, h, kind, [olders[h]], totals[h], accums, extra, lanes, [piece] * xs + outs
        )
        newest[h], extras[h] = (results[:xs], results[xs:])
    (keep, send), (quad,) = extras

    hop = 1
    high = ranks // wires
    terms = [quad]
    while 2 * hop < wires:
        got = swap_bits(send, hop)
        if 4 * hop < wires:
            terms = [sum(terms[1:], terms[0])]
            terms.append(swap_bits(terms[0], hop))
        hop *= 2
        part = (wires // hop // 2, high, width)
        keep, send = small(
            functools.partial(fold_kernel, hop), [info], [keep, got],
            [f32(*part), bf16(*part)],
        )
    quad, mixed = small(mix_kernel, [], [send, *terms], [f32(1, width), bf16(high + 16, width)])
    rest = [swap_bits(quad, k * hop // 2) for k in (1, 3)] if wires > 2 else []
    mixed = swap_bits(mixed, hop)
    scale = 1.0 / float(rows * wires * tiles * xs) ** 0.5
    finished = small(
        functools.partial(finish_kernel, xs, scale), [me[None]], [keep, mixed, quad, *rest],
        [f32(high // xs + 8, width)] * xs,
    )
    finished = [finished[0]] + [to_tile(finished[i], i) for i in others]
    gram, quadratic = small(
        place_kernel, [me[None]], finished, [f32(high // xs, local_cols), f32(1, local_cols)]
    )
    quadratic = quadratic[0]

    sums_back = [totals[0][0], totals[1][0]]
    sums_back += [to_tile(totals[1][i], i) for i in others]
    before_back = [fields[0], fields[1]]
    before_back += [to_tile(befores[i - 1], i) for i in others]
    newest_back = [newest[0][0], newest[1][0]]
    for i in others:
        newest_back += [to_tile(newest[h][i], i) for h in range(halves)]

    def paired(start):
        return [[(start, 0), (start + 1, 0)]] + [
            [(start + 1 + i, 0), (start + 1 + i, width)] for i in others
        ]

    shape = current.shape
    (before,) = small(
        functools.partial(before_kernel, paired(0)), [me[None]], before_back,
        [bf16(*shape)],
    )
    late = [[(2 * i, 0), (2 * i + 1, 0)] for i in everyone]
    arrays, lanes = (list(newest_back), [late])
    for group in (before_back, sums_back):
        lanes.append(paired(len(arrays)))
        arrays += group
    lanes.append([[(len(arrays) + i, h * width) for h in range(halves)] for i in everyone])
    arrays += starts
    last, total = small(
        functools.partial(last_kernel, *lanes), [me[None]], [coefs] + arrays,
        [bf16(*shape), f32(*shape)],
    )
    return (last, before, total, gram, quadratic)


def solution(mesh):
    return jax.shard_map(
        program,
        mesh=mesh,
        in_specs=(
            P(("sample", "wire"), "xsec", None, None),
            P(("sample", "wire"), "xsec", None),
            P(("sample", "wire"), "xsec", None, None, "cols"),
            P(("sample", "wire"), "xsec", None, None, "cols"),
            P(("sample", "wire"), "xsec", None, None, "cols"),
            P(),
            P(("sample", "wire"), "xsec", None, None),
            P(("sample", "wire"), "xsec", None, "cols"),
        ),
        out_specs=(
            P(("sample", "wire"), "xsec", None, None, "cols"),
            P(("sample", "wire"), "xsec", None, None, "cols"),
            P(("sample", "wire"), "xsec", None, None, "cols"),
            P(("sample", "wire", "xsec"), "cols"),
            P(("sample", "cols")),
        ),
        check_vma=False,
    )
```

```python
import functools

import jax
import jax.numpy as jnp
from jax import lax
from jax.experimental import pallas as pl
from jax.experimental.pallas import tpu as pltpu
from jax.sharding import PartitionSpec as P

STEPS = 4
VMEM = 12 << 20
SCALAR = pl.BlockSpec(memory_space=pltpu.SMEM)
WHOLE = pl.BlockSpec(memory_space=pltpu.VMEM)
PARAMS = pltpu.CompilerParams(vmem_limit_bytes=VMEM)


def bf16(*shape):
    return jax.ShapeDtypeStruct(shape, jnp.bfloat16)


def f32(*shape):
    return jax.ShapeDtypeStruct(shape, jnp.float32)


def cost(moved, flops=0):
    return pl.CostEstimate(flops=flops, transcendentals=0, bytes_accessed=moved)


def from_tile(x, offset, axis="xsec"):
    size = lax.axis_size(axis)
    return lax.ppermute(x, axis, [((i + offset) % size, i) for i in range(size)])


def to_tile(x, offset):
    return from_tile(x, lax.axis_size("xsec") - offset)


def around(x):
    size = lax.axis_size("wire")
    first, second = ([], [])
    for i in range(0, size, 2):
        j, k = (i + 1, (i + 2) % size)
        first += [(i, j), (j, i)]
        second += [(j, k), (k, j)]
    one = lax.ppermute(x, "wire", first)
    two = lax.ppermute(x, "wire", second)
    return one, two


def swap_bits(x, hop):
    return lax.ppermute(x, "wire", [(i, i ^ hop) for i in range(lax.axis_size("wire"))])


def own_block(me, value, offset, count):
    width = value.shape[1] // count
    picked = value[:, :width]
    for b in range(1, count):
        block = value[:, b * width : (b + 1) * width]
        picked = jnp.where((me[0] - offset + count) % count == b, block, picked)
    return picked


def half_of(x, h):
    cells, _, orbs, _, columns = x.shape
    return x[...].astype(jnp.float32)[:, 0, :, h, :].reshape(cells * orbs, columns)


def deal_kernel(offsets, count, me, x, *outs):
    width = x.shape[4] // count
    for h in range(x.shape[3]):
        value = half_of(x, h)
        for offset, out in zip(offsets, outs):
            picked = own_block(me, value, offset, count)
            out[:, h * width : (h + 1) * width] = picked.astype(x.dtype)


def deal(x, me, offsets):
    count = lax.axis_size("xsec")
    cells, _, orbs, halves, columns = x.shape
    shape = (cells * orbs, halves * columns // count)
    return small(
        functools.partial(deal_kernel, offsets, count),
        [me],
        [x],
        [jax.ShapeDtypeStruct(shape, x.dtype)] * len(offsets),
    )


def stack_kernel(*refs):
    count = len(refs) - 2
    width = refs[-1].shape[1]
    rows = refs[0].shape[0]
    for h, out in enumerate(refs[count:]):
        for i, ref in enumerate(refs[:count]):
            out[i * rows : (i + 1) * rows] = ref[:, h * width : (h + 1) * width]


def rest_kernel(me, sketch, signs, turned, own, *outs):
    cells, _, orbs, ranks = sketch.shape
    count = len(outs) + 1
    rows = cells * orbs
    width = own.shape[1]
    flipped = sketch[...].reshape(rows, ranks).astype(jnp.float32).T.astype(jnp.bfloat16)
    turned[...] = flipped
    value = (2 * signs[...] - 1).astype(jnp.float32).reshape(rows, signs.shape[3])
    own[...] = own_block(me, value, 0, count).astype(jnp.bfloat16)
    for i, out in enumerate(outs):
        out[:ranks] = flipped
        picked = own_block(me, value, i + 1, count).astype(jnp.bfloat16)
        for j in range(rows // width):
            out[ranks:, j * width : (j + 1) * width] = picked[j * width : (j + 1) * width]


def joined(me, refs, lanes, h, b, rows, width, start=0):
    value = None
    for i in range(len(lanes)):
        ref, lane = (refs[lanes[i][h][0]], lanes[i][h][1])
        part = ref[pl.ds(start, rows), lane : lane + width]
        here = (me[0] - i + len(lanes)) % len(lanes) == b
        value = part if value is None else jnp.where(here, part, value)
    return value


def before_kernel(lanes, me, *refs):
    out = refs[-1]
    cells, _, orbs, halves, columns = out.shape
    width = columns // len(lanes)
    for b in range(len(lanes)):
        both = [
            joined(me, refs, lanes, h, b, cells * orbs, width).reshape(cells, orbs, width)
            for h in range(halves)
        ]
        out[:, 0, :, :, b * width : (b + 1) * width] = jnp.stack(both, axis=2)


def last_kernel(late_lanes, mid_lanes, sum_lanes, start_lanes, me, coef, *refs):
    newest, summed = refs[-2:]
    _, _, orbs, halves, columns = newest.shape
    count = len(late_lanes)
    width = columns // count
    low = pl.multiple_of(pl.program_id(0) * orbs, orbs)
    for b in range(count):
        at = slice(b * width, (b + 1) * width)
        lates = []
        for h in range(halves):
            late, mid, total, start = [
                joined(me, refs, lanes, h, b, orbs, width, low)
                for lanes in (late_lanes, mid_lanes, sum_lanes, start_lanes)
            ]
            lates.append(late)
            late, mid = (late.astype(jnp.float32), mid.astype(jnp.float32))
            total = start + total + coef[:, STEPS - 2 : STEPS - 1] * mid
            summed[0, 0, :, h, at] = total + coef[:, STEPS - 1 : STEPS] * late
        newest[0, 0, :, :, at] = jnp.stack(lates, axis=1)


def pack_kernel(core, me, pattern, blocks, out):
    share, orbs, wide = blocks.shape
    span = wide // orbs // 3
    slots = out.shape[2] // orbs // span
    zero = jnp.zeros((orbs, orbs), jnp.bfloat16)
    for c in range(share):
        cell = core[0] * share + c

        def block(d, e):
            column = 3 * d + e
            value = blocks[c, :, column * orbs : (column + 1) * orbs]
            return jnp.where(pattern[cell, column] != 0, value, zero)

        for d in range(span):
            values = [block(d, e) for e in range(3)]
            if slots == 2:
                values = [values[1], jnp.where(me[0] == 0, values[2], values[0])]
            for n, value in enumerate(values):
                at = (slots * d + n) * orbs
                out[c, :, at : at + orbs] = value


def packed(blocks, pattern, core, me, cores, slots):
    cells, orbs, wide = blocks.shape
    share = cells // cores
    shape = (share, orbs, wide // 3 * slots)
    return pl.pallas_call(
        pack_kernel,
        out_shape=bf16(*shape),
        grid_spec=pltpu.PrefetchScalarGridSpec(
            num_scalar_prefetch=3,
            grid=(1,),
            in_specs=[pl.BlockSpec((share, orbs, wide), lambda i, core, me, p: (core[0], 0, 0))],
            out_specs=pl.BlockSpec(shape, lambda i, core, me, p: (0, 0, 0)),
        ),
        compiler_params=PARAMS,
        cost_estimate=cost(4 * share * orbs * wide),
    )(core, me, pattern, blocks)


def band_kernel(tile, sizes, me, place, slot, pattern, *refs):
    cells, orbs, reach, tiles, pieces = sizes
    first, own, second = refs[-3:]
    share = cells // pieces
    span = 2 * reach + 1
    zero = jnp.zeros((orbs, orbs), jnp.bfloat16)
    slots = refs[0].shape[2] // orbs // span
    masked = tile == 0

    def write(parts):
        def block(c, u, x):
            d = x - c
            if d < 0 or d >= span:
                return zero
            ref = parts[c // share]

            def at(e):
                column = slots * d + e
                value = ref[c % share, :, column * orbs : (column + 1) * orbs]
                if masked:
                    value = jnp.where(pattern[c, column] != 0, value, zero)
                return value

            if slots == 2:
                return at(0 if u == tile else 1)
            if u == tile:
                return at(1)
            gap = lax.rem(me[0] + u, tiles) - lax.rem(me[0] + tile, tiles) + 1
            return jnp.where(gap == 0, at(0), jnp.where(gap == 2, at(2), zero))

        turn = lax.rem(place[0], 2) == 0
        for c in range(cells):
            rows = slice(c * orbs, (c + 1) * orbs)
            for u in range(tiles):
                for j in range(cells):
                    at = (u * cells + j) * orbs
                    own[rows, at : at + orbs] = block(c, u, reach + j)
                for j in range(reach):
                    at = (u * reach + j) * orbs
                    left, right = (block(c, u, j), block(c, u, reach + cells + j))
                    first[rows, at : at + orbs] = jnp.where(turn, right, left)
                    second[rows, at : at + orbs] = jnp.where(turn, left, right)

    if pieces == 1:
        write(refs[:1])
        return
    for k in range(pieces):

        @pl.when(slot[0] == k)
        def _():
            write([refs[(piece - k) % pieces] for piece in range(pieces)])


def band_rows(tile, parts, pattern, me, place, slot, sizes, held):
    cells, orbs, reach, tiles, _ = sizes
    rows = cells * orbs
    shapes = [(tiles * rows, tiles * n * orbs) for n in (reach, cells, reach)]
    n_in = 4 + len(parts)
    return pl.pallas_call(
        functools.partial(band_kernel, tile, sizes),
        out_shape=[bf16(*s) for s in shapes],
        grid=(1,),
        in_specs=[SCALAR] * 4
        + [pl.BlockSpec(p.shape, lambda i: (0, 0, 0)) for p in parts]
        + [pl.BlockSpec(memory_space=pl.ANY)] * len(held),
        out_specs=[pl.BlockSpec((rows, s[1]), lambda i: (tile, 0)) for s in shapes],
        input_output_aliases={n_in + i: i for i in range(len(held))},
        compiler_params=PARAMS,
        cost_estimate=cost(4 * rows * tiles * 3 * cells * orbs),
    )(me, place, slot, pattern, *parts, *held)


def step_kernel(step, tiles, width, counts, lanes, kind, *refs):
    refs = list(refs)

    def take(n):
        taken = refs[:n]
        del refs[:n]
        return taken

    place = take(1)[0] if kind == "sketch" else None
    own, first, second = take(3)
    coef = take(1)[0] if kind in ("sum", "sketch", "probe") else None
    field, near, far, older, sums, start, extra = [take(n) for n in counts]
    outs = refs

    def parts(group, lane):
        return [ref[:, low : low + width] for ref, low in zip(group, lane)]

    image = None
    for band, group in zip((own, first, second), (field, near, far)):
        at = 0
        for ref in group:
            depth = ref.shape[0]
            term = jnp.dot(
                band[:, at : at + depth], ref[...], preferred_element_type=jnp.float32
            )
            image = term if image is None else image + term
            at += depth

    old = jnp.concatenate(parts(older, lanes[0])).astype(jnp.float32)
    value = (2.0 * image - old).astype(jnp.bfloat16)
    rows = value.shape[0] // tiles

    if kind in ("plain", "sum", "before"):
        outs.pop(0)[...] = value
    if kind in ("sum", "sketch", "probe"):
        now = jnp.concatenate([ref[...] for ref in field]).astype(jnp.float32)
        total = coef[:, step - 1 : step] * now + coef[:, step : step + 1] * value.astype(jnp.float32)
        if sums:
            total = jnp.concatenate(parts(start, lanes[2])) + jnp.concatenate(parts(sums, lanes[1])) + total
    if kind == "sum":
        for i, out in enumerate(outs):
            mine = total[i * rows : (i + 1) * rows]
            if out.shape[1] == width:
                out[...] = mine
            else:
                out[:, :width] = extra[i - 1][...]
                out[:, width:] = mine
    if kind == "before":
        for i, out in enumerate(outs):
            at = slice((i + 1) * rows, (i + 2) * rows)
            out[:, :width] = extra[0][at]
            out[:, width:] = value[at]
    if kind in ("sketch", "probe"):
        for i in range(len(extra)):
            outs.pop(0)[...] = value[i * rows : (i + 1) * rows]
    if kind == "sketch":
        sketched = total.astype(jnp.bfloat16)
        keep, send = outs
        high = keep.shape[1]
        ranks = 2 * keep.shape[0] * high
        piece = None
        for i, omega in enumerate(extra):
            term = jnp.dot(
                omega[:ranks],
                sketched[i * rows : (i + 1) * rows],
                preferred_element_type=jnp.float32,
            )
            piece = term if piece is None else piece + term
        odd = place[0] % 2 == 1
        for q in range(keep.shape[0]):
            low = piece[2 * q * high : (2 * q + 1) * high]
            top = piece[(2 * q + 1) * high : (2 * q + 2) * high]
            keep[q] = jnp.where(odd, top, low)
            send[q] = jnp.where(odd, low, top).astype(jnp.bfloat16)
    if kind == "probe":
        signs = [extra[0][...]]
        for ref in extra[1:]:
            ranks = ref.shape[0] - width
            signs += [ref[ranks:, j * width : (j + 1) * width] for j in range(rows // width)]
        signs = jnp.concatenate(signs).astype(jnp.float32)
        outs[0][...] = jnp.sum(signs * total, axis=0, keepdims=True)


def advance(step, width, kind, scalars, coefs, band, groups, lanes, outs):
    tiles = lax.axis_size("xsec")
    flat = coefs + [x for group in groups for x in group]
    rows, depth = band[1].shape
    return pl.pallas_call(
        functools.partial(
            step_kernel, step, tiles, width, [len(group) for group in groups], lanes, kind
        ),
        out_shape=outs,
        in_specs=[SCALAR] * len(scalars) + [WHOLE] * (3 + len(flat)),
        out_specs=[WHOLE] * len(outs),
        compiler_params=PARAMS,
        cost_estimate=cost(6 * rows * depth, 6 * rows * depth * width),
    )(*scalars, band[1], band[0], band[2], *flat)


def fold_kernel(hop, place, keep, got, kept, send):
    odd = (place[0] // hop) % 2 == 1
    for q in range(kept.shape[0]):
        low = keep[2 * q] + got[2 * q].astype(jnp.float32)
        top = keep[2 * q + 1] + got[2 * q + 1].astype(jnp.float32)
        kept[q] = jnp.where(odd, top, low)
        send[q] = jnp.where(odd, low, top).astype(jnp.bfloat16)


def mix_kernel(send, *refs):
    terms, (quad, out) = (refs[:-2], refs[-2:])
    rows = send.shape[1]
    total = terms[0][...]
    for term in terms[1:]:
        total = total + term[...]
    quad[...] = total
    high = total.astype(jnp.bfloat16)
    low = (total - high.astype(jnp.float32)).astype(jnp.bfloat16)
    spare = out.shape[0] - rows - 2
    pad = jnp.zeros((spare, total.shape[1]), jnp.float32)
    tail = jnp.concatenate([high.astype(jnp.float32), low.astype(jnp.float32), pad])
    out[:rows] = send[0]
    out[rows:] = tail.astype(jnp.bfloat16)


def finish_kernel(count, scale, me, keep, got, quad, *refs):
    rest, outs = (refs[:-count], refs[-count:])
    rows = keep.shape[1]
    share = rows // count
    tail = got[rows:].astype(jnp.float32)
    total = quad[...] + tail[0:1] + tail[1:2]
    for term in rest:
        total = total + term[...]
    total = total * scale
    spare = jnp.zeros((outs[0].shape[0] - share - 1, total.shape[1]), jnp.float32)
    gram = (keep[0] + got[:rows].astype(jnp.float32)) * scale
    for i in range(count):
        picked = gram[:share]
        for b in range(1, count):
            here = (me[0] + i) % count == b
            picked = jnp.where(here, gram[b * share : (b + 1) * share], picked)
        outs[i][:share] = picked
        outs[i][share:] = jnp.concatenate([total, spare])


def place_kernel(me, *refs):
    parts, (gram, quad) = (refs[:-2], refs[-2:])
    count = len(parts)
    share, columns = gram.shape
    width = columns // count
    for b in range(count):
        value = parts[0][...]
        for i in range(1, count):
            value = jnp.where((me[0] - i + count) % count == b, parts[i][...], value)
        gram[:, b * width : (b + 1) * width] = value[:share]
        quad[:, b * width : (b + 1) * width] = value[share : share + 1]


def small(kernel, scalars, arrays, outs):
    return pl.pallas_call(
        kernel,
        out_shape=outs,
        in_specs=[SCALAR] * len(scalars) + [WHOLE] * len(arrays),
        out_specs=[WHOLE] * len(outs),
        compiler_params=PARAMS,
        cost_estimate=cost(sum(4 * x.size for x in arrays)),
    )(*scalars, *arrays)


def program(blocks, pattern, current, previous, accum, coefs, sketch, signs):
    cells, tiles, orbs, wide = blocks.shape
    halves, local_cols = current.shape[3:]
    reach = wide // orbs // 6
    xs, me = (lax.axis_size("xsec"), lax.axis_index("xsec").astype(jnp.int32))
    wires, place = (lax.axis_size("wire"), lax.axis_index("wire").astype(jnp.int32))
    cores, core = (lax.axis_size("cols"), lax.axis_index("cols").astype(jnp.int32))
    width = local_cols // xs
    rows = cells * orbs
    others = range(1, xs)
    assert tiles == 1 and cells == reach and wires % 2 == 0 and cells % cores == 0
    assert halves == 2 and STEPS == 4

    everyone = range(xs)
    coefs = coefs[None]
    assert rows % width == 0

    leaving = deal(current, me[None], others)
    coming = [from_tile(leaving[i - 1], i) for i in others]
    staying = deal(current, me[None], [0])
    fields = small(stack_kernel, [], [*staying, *coming], [bf16(xs * rows, width)] * halves)

    blocks = blocks[:, 0]
    pattern = pattern[:, 0]
    mine = packed(blocks, pattern, core[None], me[None], cores, min(xs, 3))
    shares = [from_tile(mine, i) for i in others]

    band = ()
    for i in range(xs):
        parts, slot, pieces = ([blocks], core[None], 1)
        if i > 0:
            parts = [shares[i - 1]]
            parts += [from_tile(shares[i - 1], k, "cols") for k in range(1, cores)]
            slot, pieces = (core[None], cores)
        sizes = (cells, orbs, reach, xs, pieces)
        band = band_rows(i, parts, pattern, me[None], place[None], slot, sizes, band)

    dealt = deal(previous, me[None], everyone)
    older = [dealt[0]] + [from_tile(dealt[i], i) for i in others]
    dealt = deal(accum, me[None], everyone)
    starts = dealt
    accums = [dealt[0]] + [from_tile(dealt[i], i) for i in others]
    ranks = sketch.shape[3]
    turned, signed, *leaving = small(
        rest_kernel, [me[None]], [sketch, signs],
        [bf16(ranks, rows), bf16(rows, width)] + [bf16(ranks + width, rows)] * (xs - 1),
    )
    coming = [from_tile(leaving[i - 1], i) for i in others]
    omega, signed = ([turned, *coming], [signed, *coming])

    full = bf16(xs * rows, width)
    piece = bf16(rows, width)
    info = place[None]
    fields = list(fields)
    olders, totals = ([None] * halves, [None] * halves)
    zero = (0,) * xs

    def run(step, h, kind, older, sums, start, extra, lanes, outs):
        near, far = around(fields[h])
        scalars = [info] if kind == "sketch" else []
        weights = [coefs] if kind in ("sum", "sketch", "probe") else []
        return advance(
            step, width, kind, scalars, weights, band,
            ([fields[h]], [near], [far], older, sums, start, extra), lanes, outs,
        )

    for h in range(halves):
        (nxt,) = run(0, h, "plain", older, [], [], [], ((h * width,) * xs, (), ()), [full])
        olders[h], fields[h] = (fields[h], nxt)
    for h in range(halves):
        extra = totals[0][1:] if h else []
        outs = [full, f32(rows, width)] + [f32(rows, (h + 1) * width)] * (xs - 1)
        nxt, *totals[h] = run(
            1, h, "sum", [olders[h]], [], [], extra, (zero, (), ()), outs
        )
        olders[h], fields[h] = (fields[h], nxt)
    for h in range(halves):
        kind, extra, outs = ("plain", [], [])
        if h:
            kind, extra, outs = ("before", [fields[0]], [bf16(rows, 2 * width)] * (xs - 1))
        nxt, *befores = run(2, h, kind, [olders[h]], [], [], extra, (zero, (), ()), [full] + outs)
        olders[h], fields[h] = (fields[h], nxt)
    newest, extras = ([None] * halves, [None] * halves)
    part = (wires // 2, ranks // wires, width)
    ends = [("sketch", omega, [f32(*part), bf16(*part)]), ("probe", signed, [f32(1, width)])]
    for h in range(halves):
        kind, extra, outs = ends[h]
        lanes = (zero, (0,) + (h * width,) * (xs - 1), (h * width,) * xs)
        results = run(
            3, h, kind, [olders[h]], totals[h], accums, extra, lanes, [piece] * xs + outs
        )
        newest[h], extras[h] = (results[:xs], results[xs:])
    (keep, send), (quad,) = extras

    hop = 1
    high = ranks // wires
    terms = [quad]
    while 2 * hop < wires:
        got = swap_bits(send, hop)
        if 4 * hop < wires:
            terms = [sum(terms[1:], terms[0])]
            terms.append(swap_bits(terms[0], hop))
        hop *= 2
        part = (wires // hop // 2, high, width)
        keep, send = small(
            functools.partial(fold_kernel, hop), [info], [keep, got],
            [f32(*part), bf16(*part)],
        )
    quad, mixed = small(mix_kernel, [], [send, *terms], [f32(1, width), bf16(high + 16, width)])
    rest = [swap_bits(quad, k * hop // 2) for k in (1, 3)] if wires > 2 else []
    mixed = swap_bits(mixed, hop)
    scale = 1.0 / float(rows * wires * tiles * xs) ** 0.5
    finished = small(
        functools.partial(finish_kernel, xs, scale), [me[None]], [keep, mixed, quad, *rest],
        [f32(high // xs + 8, width)] * xs,
    )
    finished = [finished[0]] + [to_tile(finished[i], i) for i in others]
    gram, quadratic = small(
        place_kernel, [me[None]], finished, [f32(high // xs, local_cols), f32(1, local_cols)]
    )
    quadratic = quadratic[0]

    sums_back = [totals[0][0], totals[1][0]]
    sums_back += [to_tile(totals[1][i], i) for i in others]
    before_back = [fields[0], fields[1]]
    before_back += [to_tile(befores[i - 1], i) for i in others]
    newest_back = [newest[0][0], newest[1][0]]
    for i in others:
        newest_back += [to_tile(newest[h][i], i) for h in range(halves)]

    def paired(start):
        return [[(start, 0), (start + 1, 0)]] + [
            [(start + 1 + i, 0), (start + 1 + i, width)] for i in others
        ]

    shape = current.shape
    (before,) = small(
        functools.partial(before_kernel, paired(0)), [me[None]], before_back,
        [bf16(*shape)],
    )
    late = [[(2 * i, 0), (2 * i + 1, 0)] for i in everyone]
    arrays, lanes = (list(newest_back), [late])
    for group in (before_back, sums_back):
        lanes.append(paired(len(arrays)))
        arrays += group
    lanes.append([[(len(arrays) + i, h * width) for h in range(halves)] for i in everyone])
    arrays += starts
    cell = pl.BlockSpec((1,) + shape[1:], lambda i: (i, 0, 0, 0, 0))
    last, total = pl.pallas_call(
        functools.partial(last_kernel, *lanes),
        out_shape=[bf16(*shape), f32(*shape)],
        grid=(cells,),
        in_specs=[SCALAR] + [WHOLE] * (1 + len(arrays)),
        out_specs=[cell, cell],
        compiler_params=PARAMS,
        cost_estimate=cost(16 * current.size),
    )(me[None], coefs, *arrays)
    return (last, before, total, gram, quadratic)


def solution(mesh):
    return jax.shard_map(
        program,
        mesh=mesh,
        in_specs=(
            P(("sample", "wire"), "xsec", None, None),
            P(("sample", "wire"), "xsec", None),
            P(("sample", "wire"), "xsec", None, None, "cols"),
            P(("sample", "wire"), "xsec", None, None, "cols"),
            P(("sample", "wire"), "xsec", None, None, "cols"),
            P(),
            P(("sample", "wire"), "xsec", None, None),
            P(("sample", "wire"), "xsec", None, "cols"),
        ),
        out_specs=(
            P(("sample", "wire"), "xsec", None, None, "cols"),
            P(("sample", "wire"), "xsec", None, None, "cols"),
            P(("sample", "wire"), "xsec", None, None, "cols"),
            P(("sample", "wire", "xsec"), "cols"),
            P(("sample", "cols")),
        ),
        check_vma=False,
    )
```
